32 devices in a mesh: row: 4 (over y, x), col: 8 (over z, core).
Axes of the slice: x: 2, y: 2, z: 4, core: 2. Of those that a mesh axis runs over, the one named last changes fastest.
Arguments:
- image: bfloat16 [64, 256, 768], P('row', 'col'), may hold values from -6 to 6
- conv_taps: float32 [9, 768], replicated, may hold values from -0.5 to 0.5
- w_query: bfloat16 [768, 768], replicated, may hold values from -0.21875 to 0.21875
- w_key: bfloat16 [768, 768], replicated, may hold values from -0.21875 to 0.21875
- w_value: bfloat16 [768, 768], replicated, may hold values from -0.21875 to 0.21875
- w_out: bfloat16 [768, 768], replicated, may hold values from -0.21875 to 0.21875
- grad_out: bfloat16 [64, 256, 768], P('row', 'col'), may hold values from -6 to 6
Outputs:
- grad_image: bfloat16 [64, 256, 768], P('row', 'col')
- grad_weights: float32 [768, 3072], P(None, 'col')
- grad_conv: float32 [9, 768], P(None, 'col')
The draws below stay inside these ranges and needn't reach their ends.
All inputs are finite; a program needn't handle non-finite values.
Results may differ from the reference program's by a relative error of at most 0.022.
Values may be sent and summed in bfloat16 or wider, within the bound.
A program may use at most 128 MiB of HBM per device.

```python
import math
from functools import partial
import jax
import jax.numpy as jnp
from jax import lax

C = 768
HEADS = 12
HD = 64
POOL = 8
H = 64
W = 256
N_ROW = 4


def raised(drawn, own_key, source, target, blocks, factor):
    def block_of(axis_at):
        return (jnp.arange(drawn.shape[axis_at]) // (drawn.shape[axis_at] // blocks)).reshape((-1,) + (1,) * (drawn.ndim - 1 - axis_at))

    near = jax.random.permutation(own_key, blocks)[block_of(target)]
    second = (block_of(target) + blocks // 2) % blocks
    return jnp.where((block_of(source) == near) | (block_of(source) == second), factor * drawn, drawn)


def shard_levels(own_key, dims, cuts, smallest, largest):
    def one(dim, shards_of):
        steps = jax.random.uniform(jax.random.fold_in(jax.random.fold_in(own_key, 6), dim), (shards_of,), jnp.float32, smallest / len(cuts), largest / len(cuts))
        return jnp.repeat(jnp.exp(steps), dims[dim] // shards_of).reshape((-1,) + (1,) * (len(dims) - dim - 1))

    level = one(*cuts[0])
    for cut in cuts[1:]:
        level = level * one(*cut)
    return level


def noise(stream_key, shape, scale, reach, shards=(), kind=jnp.bfloat16):
    values = jax.random.normal(stream_key, shape, jnp.float32) * scale
    if len(shards) > 0:
        values = shard_levels(stream_key, shape, shards, -0.22, 0.18) * values
    return jnp.clip(values, min=-reach, max=reach).astype(kind)


def noise_with(key, shape, scale, reach, split, heavy, kind=jnp.bfloat16):
    values = scale * jax.random.normal(key, shape, jnp.float32)
    if split:
        values = values * shard_levels(key, shape, split, -0.22, 0.18)
    return jnp.clip(raised(values, jax.random.fold_in(key, 3), *heavy), -reach, reach).astype(kind)


def setup_inputs(seed: int = 0) -> dict:
    arg_keys = jax.random.split(jax.random.key(seed), 8)
    image = noise(arg_keys[0], (H, W, C), 1.0, 6.0, ((0, 4), (1, 8)))
    conv_taps = jnp.clip(jax.random.uniform(arg_keys[1], (9, C), jnp.float32, -0.5, 0.5), -0.5, 0.5)
    w_query = noise(arg_keys[2], (C, C), C ** -0.5, 0.21875)
    w_key = noise(arg_keys[3], (C, C), C ** -0.5, 0.21875)
    w_value = noise(arg_keys[4], (C, C), C ** -0.5, 0.21875)
    w_out = noise(arg_keys[5], (C, C), C ** -0.5, 0.21875)
    grad_out = noise_with(arg_keys[6], (H, W, C), 1.0, 6.0, ((0, 4), (1, 8)), (0, 2, 4, 2.0))
    return dict(image=image, conv_taps=conv_taps, w_query=w_query, w_key=w_key, w_value=w_value, w_out=w_out, grad_out=grad_out)


EPSILON = 1e-05

def contract_first(left, right):
    return lax.dot_general(left, right, (((0,), (0,)), ((), ())), preferred_element_type=jnp.float32)

def contract_last(left, right):
    return lax.dot_general(left, right, (((1,), (1,)), ((), ())), preferred_element_type=jnp.float32)

def exact_first(left, right):
    return lax.dot_general(left, right, (((0,), (0,)), ((), ())), precision=lax.Precision.HIGHEST, preferred_element_type=jnp.float32)

def exact_last(left, right):
    return lax.dot_general(left, right, (((1,), (1,)), ((), ())), precision=lax.Precision.HIGHEST, preferred_element_type=jnp.float32)

def stencil(padded, taps, height, width, flipped):
    total = jnp.zeros((height, width, padded.shape[2]), jnp.float32)
    for tap_row in range(3):
        for tap_col in range(3):
            if flipped:
                window = padded[2 - tap_row:2 - tap_row + height, 2 - tap_col:2 - tap_col + width]
            else:
                window = padded[tap_row:tap_row + height, tap_col:tap_col + width]
            total = total + taps[3 * tap_row + tap_col] * window.astype(jnp.float32)
    return total

def attend(carry, inputs, key_heads, value_heads):
    grad_key, grad_value = carry
    query_block, dout_block = inputs
    softmax_scale = HD ** (-0.5)
    query_heads = query_block.reshape(-1, HEADS, HD).astype(jnp.float32)
    dout_heads = dout_block.reshape(-1, HEADS, HD).astype(jnp.float32)
    key_float = key_heads.astype(jnp.float32)
    value_float = value_heads.astype(jnp.float32)
    scores = jnp.einsum('qhd,khd->hqk', query_heads, key_float) * softmax_scale
    expons = jnp.exp(scores)
    probabilities = expons / lax.optimization_barrier(jnp.sum(expons, axis=-1, keepdims=True))
    weights = probabilities.astype(jnp.bfloat16)
    attended = jnp.einsum('hqk,khd->qhd', weights.astype(jnp.float32), value_float).astype(jnp.bfloat16)
    grad_probs = jnp.einsum('qhd,khd->hqk', dout_heads, value_float)
    deltas = jnp.einsum('qhd,qhd->hq', dout_heads, attended.astype(jnp.float32))
    grad_scores = (probabilities * (grad_probs - deltas[:, :, None]) * softmax_scale).astype(jnp.bfloat16)
    grad_query = jnp.einsum('hqk,khd->qhd', grad_scores.astype(jnp.float32), key_float).astype(jnp.bfloat16)
    grad_key = grad_key + jnp.einsum('hqk,qhd->khd', grad_scores.astype(jnp.float32), query_heads)
    grad_value = grad_value + jnp.einsum('hqk,qhd->khd', weights.astype(jnp.float32), dout_heads)
    return ((grad_key, grad_value), (attended.reshape(query_block.shape), grad_query.reshape(query_block.shape)))

def reference(image, conv_taps, w_query, w_key, w_value, w_out, grad_out):
    height, width, channels = image.shape
    padded = jnp.pad(image, ((1, 1), (1, 1), (0, 0)))
    mixed = image.astype(jnp.float32) + stencil(padded, conv_taps, height, width, False)
    hidden = mixed.astype(jnp.bfloat16)
    flat_hidden = hidden.reshape(-1, channels)
    query = jnp.dot(flat_hidden, w_query, preferred_element_type=jnp.float32).astype(jnp.bfloat16)
    pooled = hidden.astype(jnp.float32).reshape(height // POOL, POOL, width // POOL, POOL, channels).mean(axis=(1, 3))
    centre = lax.optimization_barrier(jnp.mean(pooled, axis=-1, keepdims=True))
    spread = lax.optimization_barrier(jnp.mean(jnp.square(pooled - centre), axis=-1, keepdims=True))
    inverse = lax.rsqrt(spread + EPSILON)
    standard = (pooled - centre) * inverse
    normed = standard.astype(jnp.bfloat16)
    cells = normed.reshape(-1, channels)
    keys = jnp.dot(cells, w_key, preferred_element_type=jnp.float32).astype(jnp.bfloat16)
    values = jnp.dot(cells, w_value, preferred_element_type=jnp.float32).astype(jnp.bfloat16)
    flat_grad = grad_out.reshape(-1, channels)
    dout = contract_last(flat_grad, w_out).astype(jnp.bfloat16)
    row_queries = query.reshape(N_ROW, -1, channels)
    row_dout = dout.reshape(N_ROW, -1, channels)
    row_keys = keys.reshape(N_ROW, -1, HEADS, HD)
    row_values = values.reshape(N_ROW, -1, HEADS, HD)
    block_rows = math.gcd(row_queries.shape[1], 512)
    blocks = row_queries.shape[1] // block_rows

    def one_row(inputs):
        queries_row, dout_row, keys_row, values_row = inputs
        empty_grad = jnp.zeros(keys_row.shape, jnp.float32)
        carry, produced = lax.scan(partial(attend, key_heads=keys_row, value_heads=values_row), (empty_grad, empty_grad), (queries_row.reshape(blocks, block_rows, channels), dout_row.reshape(blocks, block_rows, channels)))
        return (carry[0], carry[1], produced[0].reshape(-1, channels), produced[1].reshape(-1, channels))
    grad_key, grad_value, attended, grad_query = lax.map(one_row, (row_queries, row_dout, row_keys, row_values))
    attended = attended.reshape(-1, channels)
    grad_query = grad_query.reshape(-1, channels)
    grad_key = grad_key.reshape(-1, channels)
    grad_value = grad_value.reshape(-1, channels)
    grad_wout = contract_first(attended, flat_grad)
    grad_wquery = contract_first(flat_hidden, grad_query)
    grad_hidden = contract_last(grad_query, w_query)
    cells_float = cells.astype(jnp.float32)
    grad_wkey = exact_first(cells_float, grad_key)
    grad_wvalue = exact_first(cells_float, grad_value)
    grad_normed = exact_last(grad_key, w_key.astype(jnp.float32)) + exact_last(grad_value, w_value.astype(jnp.float32))
    grad_normed = grad_normed.reshape(normed.shape)
    grad_pooled = (grad_normed - lax.optimization_barrier(jnp.mean(grad_normed, axis=-1, keepdims=True)) - standard * lax.optimization_barrier(jnp.mean(grad_normed * standard, axis=-1, keepdims=True))) * inverse
    pooled_rows, pooled_cols = (grad_pooled.shape[0], grad_pooled.shape[1])
    spread_back = jnp.broadcast_to((grad_pooled / (POOL * POOL))[:, None, :, None, :], (pooled_rows, POOL, pooled_cols, POOL, channels)).reshape(height, width, channels)
    grad_mixed = grad_out.astype(jnp.float32) + grad_hidden.reshape(height, width, channels) + spread_back
    grad_padded = jnp.pad(grad_mixed, ((1, 1), (1, 1), (0, 0)))
    grad_image = (grad_mixed + stencil(grad_padded, conv_taps, height, width, True)).astype(jnp.bfloat16)
    tap_list = []
    for tap_row in range(3):
        for tap_col in range(3):
            window = padded[tap_row:tap_row + height, tap_col:tap_col + width].astype(jnp.float32)
            tap_list.append(lax.optimization_barrier(jnp.sum(grad_mixed * window, axis=(0, 1))))
    grad_conv = jnp.stack(tap_list, axis=0)
    grad_weights = jnp.concatenate([grad_wquery, grad_wkey, grad_wvalue, grad_wout], axis=1)
    return (grad_image, grad_weights, grad_conv)
```

```python
from functools import partial
import math

import jax
import jax.numpy as jnp
from jax import lax
from jax.experimental import pallas as pl
from jax.experimental.pallas import tpu as pltpu
from jax.sharding import PartitionSpec as P

HEADS = 12
HD = 64
POOL = 8


EPSILON = 1e-05


def contract_first(left, right):
    return lax.dot_general(
        left, right, (((0,), (0,)), ((), ())), preferred_element_type=jnp.float32
    )


def contract_last(left, right):
    return lax.dot_general(
        left, right, (((1,), (1,)), ((), ())), preferred_element_type=jnp.float32
    )


def stencil(padded, taps, height, width, flipped):
    total = jnp.zeros((height, width, padded.shape[2]), jnp.float32)
    for tap_row in range(3):
        for tap_col in range(3):
            if flipped:
                window = padded[
                    2 - tap_row : 2 - tap_row + height, 2 - tap_col : 2 - tap_col + width
                ]
            else:
                window = padded[tap_row : tap_row + height, tap_col : tap_col + width]
            total = total + taps[3 * tap_row + tap_col] * window.astype(jnp.float32)
    return total


def attend(carry, inputs, key_heads, value_heads):
    grad_key, grad_value = carry
    query_block, dout_block = inputs
    softmax_scale = HD ** (-0.5)
    query_heads = query_block.reshape(-1, HEADS, HD)
    dout_heads = dout_block.reshape(-1, HEADS, HD)
    scores = (
        jnp.einsum("qhd,khd->hqk", query_heads, key_heads, preferred_element_type=jnp.float32)
        * softmax_scale
    )
    expons = jnp.exp(scores)
    probabilities = expons / jnp.sum(expons, axis=-1, keepdims=True)
    weights = probabilities.astype(jnp.bfloat16)
    attended = jnp.einsum(
        "hqk,khd->qhd", weights, value_heads, preferred_element_type=jnp.float32
    ).astype(jnp.bfloat16)
    grad_probs = jnp.einsum(
        "qhd,khd->hqk", dout_heads, value_heads, preferred_element_type=jnp.float32
    )
    deltas = jnp.einsum("qhd,qhd->hq", dout_heads, attended, preferred_element_type=jnp.float32)
    grad_scores = (probabilities * (grad_probs - deltas[:, :, None]) * softmax_scale).astype(
        jnp.bfloat16
    )
    grad_query = jnp.einsum(
        "hqk,khd->qhd", grad_scores, key_heads, preferred_element_type=jnp.float32
    ).astype(jnp.bfloat16)
    grad_key = grad_key + jnp.einsum(
        "hqk,qhd->khd", grad_scores, query_heads, preferred_element_type=jnp.float32
    )
    grad_value = grad_value + jnp.einsum(
        "hqk,qhd->khd", weights, dout_heads, preferred_element_type=jnp.float32
    )
    return (
        (grad_key, grad_value),
        (attended.reshape(query_block.shape), grad_query.reshape(query_block.shape)),
    )


MESH = pl.DeviceIdType.MESH
VMEM = pl.BlockSpec(memory_space=pltpu.VMEM)
DIRECTIONS = ((-1, 0), (1, 0), (0, -1), (0, 1), (-1, -1), (-1, 1), (1, -1), (1, 1))


def remote(source, target, send, recv, row, col):
    return pltpu.make_async_remote_copy(
        src_ref=source,
        dst_ref=target,
        send_sem=send,
        recv_sem=recv,
        device_id=(row, col),
        device_id_type=MESH,
    )


def greet_line(barrier, row, col, count, along_row):
    for step in range(1, count):
        where = (lax.rem(row + step, count), col) if along_row else (row, lax.rem(col + step, count))
        pl.semaphore_signal(barrier, inc=1, device_id=where, device_id_type=MESH)


def halo_kernel(rows_n, cols_n, with_cells, *refs):
    if with_cells:
        rows, cols, corners, cells, out_rows, out_cols, out_corners, out_cells, send, recv, cell_send, cell_recv = refs
    else:
        rows, cols, corners, out_rows, out_cols, out_corners, send, recv = refs
    row, col = lax.axis_index("row"), lax.axis_index("col")
    sources = [rows.at[0], rows.at[1], cols.at[0], cols.at[1]] + [corners.at[i] for i in range(4)]
    targets = [out_rows.at[1], out_rows.at[0], out_cols.at[1], out_cols.at[0]]
    targets += [out_corners.at[3 - i] for i in range(4)]
    out_rows[...] = jnp.zeros_like(out_rows)
    out_cols[...] = jnp.zeros_like(out_cols)
    out_corners[...] = jnp.zeros_like(out_corners)

    def present(down, right):
        ok = None
        for move, at, count in ((down, row, rows_n), (right, col, cols_n)):
            if move == 0:
                continue
            here = at > 0 if move < 0 else at < count - 1
            ok = here if ok is None else jnp.logical_and(ok, here)
        return ok

    barrier = pltpu.get_barrier_semaphore()
    for down, right in DIRECTIONS:
        @pl.when(present(down, right))
        def _(down=down, right=right):
            pl.semaphore_signal(barrier, inc=1, device_id=(row + down, col + right), device_id_type=MESH)
    if with_cells:
        greet_line(barrier, row, col, cols_n, False)
    greeted = sum(present(down, right).astype(jnp.int32) for down, right in DIRECTIONS)
    pl.semaphore_wait(barrier, greeted + (cols_n - 1 if with_cells else 0))

    def edge(at):
        down, right = DIRECTIONS[at]
        return remote(sources[at], targets[at], send.at[at], recv.at[at], row + down, col + right)

    def cell(step):
        return remote(cells, out_cells.at[col], cell_send.at[step], cell_recv.at[step], row, lax.rem(col + step, cols_n))

    for at, (down, right) in enumerate(DIRECTIONS):
        @pl.when(present(down, right))
        def _(at=at):
            edge(at).start()
    if with_cells:
        out_cells[col] = cells[...]
        for step in range(1, cols_n):
            cell(step).start()
    for at, (down, right) in enumerate(DIRECTIONS):
        @pl.when(present(down, right))
        def _(at=at):
            edge(at).wait_send()

        @pl.when(present(-down, -right))
        def _(at=at):
            edge(at).wait_recv()
    if with_cells:
        for step in range(1, cols_n):
            cell(step).wait()


def halo_exchange(tile, rows_n, cols_n, identity, cells=None):
    height, width, channels = tile.shape
    rows = jnp.stack([tile[0], tile[-1]])
    cols = jnp.stack([tile[:, 0], tile[:, -1]])
    corners = jnp.broadcast_to(
        jnp.stack([tile[0, 0], tile[0, -1], tile[-1, 0], tile[-1, -1]])[:, None], (4, 16, channels)
    )
    operands = [rows, cols, corners]
    scratch = [pltpu.SemaphoreType.DMA((8,)), pltpu.SemaphoreType.DMA((8,))]
    shapes = [jax.ShapeDtypeStruct(x.shape, x.dtype) for x in operands]
    if cells is not None:
        operands.append(cells)
        shapes.append(jax.ShapeDtypeStruct((cols_n,) + cells.shape, cells.dtype))
        scratch += [pltpu.SemaphoreType.DMA((cols_n,)), pltpu.SemaphoreType.DMA((cols_n,))]
    got = pl.pallas_call(
        partial(halo_kernel, rows_n, cols_n, cells is not None),
        out_shape=shapes,
        in_specs=[VMEM] * len(operands),
        out_specs=[VMEM] * len(shapes),
        scratch_shapes=scratch,
        compiler_params=pltpu.CompilerParams(collective_id=identity, has_side_effects=True),
    )(*operands)
    out_rows, out_cols, out_corners = got[:3]
    def band(at, left, right):
        return jnp.concatenate([left[None, :1], out_rows[at][None], right[None, :1]], axis=1)
    middle = jnp.concatenate([out_cols[0][:, None], tile, out_cols[1][:, None]], axis=1)
    padded = jnp.concatenate(
        [band(0, out_corners[0], out_corners[1]), middle, band(1, out_corners[2], out_corners[3])], axis=0
    )
    return padded if cells is None else (padded, got[3])


def gather_kernel(cols_n, block, out, send, recv):
    row, col = lax.axis_index("row"), lax.axis_index("col")
    barrier = pltpu.get_barrier_semaphore()
    greet_line(barrier, row, col, cols_n, False)
    pl.semaphore_wait(barrier, cols_n - 1)
    copies = [
        remote(block, out.at[col], send.at[step], recv.at[step], row, lax.rem(col + step, cols_n))
        for step in range(1, cols_n)
    ]
    for copy in copies:
        copy.start()
    out[col] = block[...]
    for copy in copies:
        copy.wait()


def gather_cells(block, cols_n, identity):
    return pl.pallas_call(
        partial(gather_kernel, cols_n),
        out_shape=jax.ShapeDtypeStruct((cols_n,) + block.shape, block.dtype),
        in_specs=[VMEM],
        out_specs=VMEM,
        scratch_shapes=[pltpu.SemaphoreType.DMA((cols_n,)), pltpu.SemaphoreType.DMA((cols_n,))],
        compiler_params=pltpu.CompilerParams(collective_id=identity, has_side_effects=True),
    )(block)


def scatter_kernel(cols_n, blocks, out, landed, send, recv):
    row, col = lax.axis_index("row"), lax.axis_index("col")
    barrier = pltpu.get_barrier_semaphore()
    greet_line(barrier, row, col, cols_n, False)
    pl.semaphore_wait(barrier, cols_n - 1)
    copies = []
    for step in range(1, cols_n):
        owner = lax.rem(col + step, cols_n)
        copies.append(remote(blocks.at[owner], landed.at[step], send.at[step], recv.at[step], row, owner))
    for copy in copies:
        copy.start()
    total = blocks[col].astype(jnp.float32)
    for step, copy in enumerate(copies):
        copy.wait()
        total = total + landed[step + 1].astype(jnp.float32)
    out[...] = total


def scatter_sum(blocks, cols_n, identity):
    return pl.pallas_call(
        partial(scatter_kernel, cols_n),
        out_shape=jax.ShapeDtypeStruct(blocks.shape[1:], jnp.float32),
        in_specs=[VMEM],
        out_specs=VMEM,
        scratch_shapes=[
            pltpu.VMEM(blocks.shape, blocks.dtype),
            pltpu.SemaphoreType.DMA((cols_n,)),
            pltpu.SemaphoreType.DMA((cols_n,)),
        ],
        compiler_params=pltpu.CompilerParams(collective_id=identity, has_side_effects=True),
    )(blocks)


def reduce_kernel(
    rows_n, cols_n, terms, cells, taps, out, out_cells, out_taps,
    landed1, held1, landed2, held2, landed3, taps1, taps_held, taps2,
    send1, recv1, send2, recv2, send3, recv3, send4, recv4, send_cells, recv_cells,
    send_t1, recv_t1, send_t2, recv_t2,
):
    row, col = lax.axis_index("row"), lax.axis_index("col")
    chip, core = col // 2, lax.rem(col, 2)
    chips = cols_n // 2
    items = cols_n // 4
    half = items // 2
    is_cells = jnp.logical_and(chip >= half, chip < chips - half)
    is_terms = jnp.logical_or(chip < half, chip >= chips - half)
    barrier = pltpu.get_barrier_semaphore()
    greet_line(barrier, row, col, cols_n, False)
    greet_line(barrier, row, col, rows_n, True)
    pl.semaphore_wait(barrier, cols_n + rows_n - 2)

    def mate(step):
        return lax.rem(row + step, rows_n)

    def first(item):
        return remote(
            terms.at[1 - core, item], landed1.at[item], send1.at[item], recv1.at[item], row, 2 * chip + 1 - core
        )

    def second(item, step):
        return remote(
            held1.at[item, mate(step)], landed2.at[item, step - 1], send2.at[item, step - 1],
            recv2.at[item, step - 1], mate(step), col,
        )

    def owner_of(item):
        return item if item < half else chips - items + item

    def third(item):
        return remote(
            held2.at[item], landed3.at[chip], send3.at[item], recv3.at[chip], row, 2 * owner_of(item) + core
        )

    def fourth(step):
        return remote(out.at[row], out.at[row], send4.at[step - 1], recv4.at[step - 1], mate(step), col)

    def cell(step):
        return remote(
            cells, out_cells.at[row], send_cells.at[step - 1], recv_cells.at[step - 1], mate(step), col
        )

    def tap_first(step):
        owner = lax.rem(col + step, cols_n)
        return remote(taps.at[owner], taps1.at[step - 1], send_t1.at[step - 1], recv_t1.at[step - 1], row, owner)

    def tap_second(step):
        return remote(taps_held, taps2.at[step - 1], send_t2.at[step - 1], recv_t2.at[step - 1], mate(step), col)

    for item in range(items):
        first(item).start()
    for step in range(1, cols_n):
        tap_first(step).start()
    for item in range(items):
        first(item).wait_recv()
        for step in range(1, rows_n + 1):
            there = mate(step)
            held1[item, there] = (
                terms[core, item, there].astype(jnp.float32) + landed1[item, there].astype(jnp.float32)
            ).astype(held1.dtype)
            if step < rows_n:
                second(item, step).start()

    @pl.when(is_cells)
    def _():
        for step in range(1, rows_n):
            cell(step).start()

    out_cells[row] = cells[...]
    tap_total = taps[col].astype(jnp.float32)
    for step in range(1, cols_n):
        tap_first(step).wait_recv()
        tap_total = tap_total + taps1[step - 1].astype(jnp.float32)
    taps_held[...] = tap_total.astype(taps_held.dtype)
    for step in range(1, rows_n):
        tap_second(step).start()
    for item in range(items):
        total = held1[item, row].astype(jnp.float32)
        for step in range(1, rows_n):
            second(item, step).wait_recv()
            total = total + landed2[item, step - 1].astype(jnp.float32)
        held2[item] = total.astype(held2.dtype)

        @pl.when(chip != owner_of(item))
        def _(item=item):
            third(item).start()

    tap_total = taps_held[...].astype(jnp.float32)
    for step in range(1, rows_n):
        tap_second(step).wait_recv()
        tap_total = tap_total + taps2[step - 1].astype(jnp.float32)
    out_taps[...] = tap_total

    @pl.when(is_terms)
    def _():
        mine = lax.rem(chip, chips - items)
        total = held2[mine].astype(jnp.float32)
        for step in range(1, chips):
            source = lax.rem(chip + step, chips)
            remote(
                held2.at[0], landed3.at[source], send3.at[0], recv3.at[source], row, 2 * source + core
            ).wait_recv()
            total = total + landed3[source].astype(jnp.float32)
        out[row] = total.astype(out.dtype)
        for step in range(1, rows_n):
            fourth(step).start()
        for step in range(1, rows_n):
            fourth(step).wait()

    @pl.when(is_cells)
    def _():
        for step in range(1, rows_n):
            cell(step).wait()

    for item in range(items):
        first(item).wait_send()
        for step in range(1, rows_n):
            second(item, step).wait_send()

        @pl.when(chip != owner_of(item))
        def _(item=item):
            third(item).wait_send()

    for step in range(1, cols_n):
        tap_first(step).wait_send()
    for step in range(1, rows_n):
        tap_second(step).wait_send()


def reduce_all(terms, cells, taps, rows_n, cols_n, identity):
    _, items, _, high, wide = terms.shape
    chips = cols_n // 2
    kind = terms.dtype
    def sems(*shape):
        return [pltpu.SemaphoreType.DMA(shape), pltpu.SemaphoreType.DMA(shape)]
    return pl.pallas_call(
        partial(reduce_kernel, rows_n, cols_n),
        out_shape=[
            jax.ShapeDtypeStruct((rows_n, high, wide), kind),
            jax.ShapeDtypeStruct((rows_n,) + cells.shape, kind),
            jax.ShapeDtypeStruct(taps.shape[1:], jnp.float32),
        ],
        in_specs=[VMEM] * 3,
        out_specs=[VMEM] * 3,
        scratch_shapes=[
            pltpu.VMEM((items, rows_n, high, wide), kind),
            pltpu.VMEM((items, rows_n, high, wide), kind),
            pltpu.VMEM((items, rows_n - 1, high, wide), kind),
            pltpu.VMEM((items, high, wide), kind),
            pltpu.VMEM((chips, high, wide), kind),
            pltpu.VMEM((cols_n - 1,) + taps.shape[1:], kind),
            pltpu.VMEM(taps.shape[1:], kind),
            pltpu.VMEM((rows_n - 1,) + taps.shape[1:], kind),
        ]
        + sems(items)
        + sems(items, rows_n - 1)
        + [pltpu.SemaphoreType.DMA((items,)), pltpu.SemaphoreType.DMA((chips,))]
        + sems(rows_n - 1)
        + sems(rows_n - 1)
        + sems(cols_n - 1)
        + sems(rows_n - 1),
        compiler_params=pltpu.CompilerParams(collective_id=identity, has_side_effects=True),
    )(terms, cells, taps)


def split_terms(query_terms, out_terms, rows_n, cols_n, shard):
    parts = []
    for core in range(2):
        for term in (query_terms, out_terms):
            for item in range(cols_n // 8):
                at = (2 * item + core) * shard
                parts.append(term[:, at : at + shard])
    stacked = jnp.stack(parts)
    return stacked.reshape(2, cols_n // 4, rows_n, query_terms.shape[0] // rows_n, shard)


def on_device(image, conv_taps, w_query, w_key, w_value, w_out, grad_out):
    rows_n, cols_n = lax.axis_size("row"), lax.axis_size("col")
    height, width, channels = image.shape
    padded = halo_exchange(image, rows_n, cols_n, 0)
    mixed = image.astype(jnp.float32) + stencil(padded, conv_taps, height, width, False)
    hidden = mixed.astype(jnp.bfloat16)
    flat_hidden = hidden.reshape(-1, channels)
    query = jnp.dot(flat_hidden, w_query, preferred_element_type=jnp.float32).astype(jnp.bfloat16)
    pooled = (
        hidden.astype(jnp.float32)
        .reshape(height // POOL, POOL, width // POOL, POOL, channels)
        .mean(axis=(1, 3))
    )
    centre = jnp.mean(pooled, axis=-1, keepdims=True)
    spread = jnp.mean(jnp.square(pooled - centre), axis=-1, keepdims=True)
    inverse = lax.rsqrt(spread + EPSILON)
    standard = (pooled - centre) * inverse
    own_cells = standard.astype(jnp.bfloat16).reshape(-1, channels)
    own = own_cells.shape[0]
    key_cells = gather_cells(own_cells, cols_n, 1).reshape(-1, channels)
    keys = jnp.dot(key_cells, w_key, preferred_element_type=jnp.float32).astype(jnp.bfloat16)
    values = jnp.dot(key_cells, w_value, preferred_element_type=jnp.float32).astype(jnp.bfloat16)
    flat_grad = grad_out.reshape(-1, channels)
    dout = contract_last(flat_grad, w_out).astype(jnp.bfloat16)
    key_heads = keys.reshape(-1, HEADS, HD)
    value_heads = values.reshape(-1, HEADS, HD)
    empty_grad = jnp.zeros(key_heads.shape, jnp.float32)
    (grad_key, grad_value), (attended, grad_query) = attend(
        (empty_grad, empty_grad), (query, dout), key_heads, value_heads
    )
    grad_wout = contract_first(attended, flat_grad)
    grad_wquery = contract_first(flat_hidden, grad_query)
    grad_hidden = contract_last(grad_query, w_query)
    cell_grads = jnp.concatenate(
        [grad_key.reshape(cols_n, own, channels), grad_value.reshape(cols_n, own, channels)], axis=1
    ).astype(jnp.bfloat16)
    totals = scatter_sum(cell_grads, cols_n, 2)
    sent_totals = totals.astype(jnp.bfloat16)
    rest = (totals - sent_totals.astype(jnp.float32)).astype(jnp.bfloat16)
    def exact(at, weight):
        both = jnp.concatenate([sent_totals[at : at + own], rest[at : at + own]], axis=0)
        product = contract_last(both, weight)
        return product[:own] + product[own:]
    grad_normed = (exact(0, w_key) + exact(own, w_value)).reshape(standard.shape)
    grad_pooled = (
        grad_normed
        - jnp.mean(grad_normed, axis=-1, keepdims=True)
        - standard * jnp.mean(grad_normed * standard, axis=-1, keepdims=True)
    ) * inverse
    spread_back = jnp.broadcast_to(
        (grad_pooled / (POOL * POOL))[:, None, :, None, :],
        (height // POOL, POOL, width // POOL, POOL, channels),
    ).reshape(height, width, channels)
    grad_mixed = (
        grad_out.astype(jnp.float32) + grad_hidden.reshape(height, width, channels) + spread_back
    )
    grad_padded, all_totals = halo_exchange(
        grad_mixed.astype(jnp.bfloat16), rows_n, cols_n, 3, sent_totals
    )
    grad_image = (grad_mixed + stencil(grad_padded, conv_taps, height, width, True)).astype(
        jnp.bfloat16
    )
    tap_list = []
    for tap_row in range(3):
        for tap_col in range(3):
            window = padded[tap_row : tap_row + height, tap_col : tap_col + width].astype(
                jnp.float32
            )
            tap_list.append(jnp.sum(grad_mixed * window, axis=(0, 1)))
    tap_terms = jnp.stack(tap_list, axis=0)
    tap_terms = jnp.pad(tap_terms, ((0, 16 - tap_terms.shape[0]), (0, 0))).astype(jnp.bfloat16)
    tap_terms = tap_terms.reshape(16, cols_n, -1).transpose(1, 0, 2)
    shard = 4 * channels // cols_n
    quarter = cols_n // 4
    col = lax.axis_index("col")
    terms = split_terms(
        grad_wquery.astype(jnp.bfloat16), grad_wout.astype(jnp.bfloat16), rows_n, cols_n, shard
    )
    side = jnp.where(
        col < 2 * quarter,
        all_totals[:, :own].reshape(-1, channels),
        all_totals[:, own:].reshape(-1, channels),
    )
    mine = lax.dynamic_slice_in_dim(side, lax.rem(col, quarter) * shard, shard, axis=1)
    cells = jnp.concatenate([key_cells, mine], axis=1)
    summed, gathered, grad_conv = reduce_all(terms, cells, tap_terms, rows_n, cols_n, 4)
    gathered = gathered.reshape(-1, channels + shard)
    from_cells = contract_first(gathered[:, :channels], gathered[:, channels:])
    is_cells = jnp.logical_and(col >= quarter, col < cols_n - quarter)
    grad_weights = jnp.where(
        is_cells, from_cells, summed.reshape(channels, shard).astype(jnp.float32)
    )
    return (grad_image, grad_weights, grad_conv[:9])


def solution(mesh):
    return jax.shard_map(
        on_device,
        mesh=mesh,
        in_specs=(P("row", "col", None), P(), P(), P(), P(), P(), P("row", "col", None)),
        out_specs=(P("row", "col", None), P(None, "col"), P(None, "col")),
        check_vma=False,
    )
```

```python
from functools import partial

import jax
import jax.numpy as jnp
from jax import lax
from jax.experimental import pallas as pl
from jax.experimental.pallas import tpu as pltpu
from jax.sharding import PartitionSpec as P

HD = 64
POOL = 8
LANES = 128
EDGE = 8

EPSILON = 1e-05
MESH = pl.DeviceIdType.MESH
VMEM = pl.BlockSpec(memory_space=pltpu.VMEM)
DIRECTIONS = ((-1, 0), (1, 0), (0, -1), (0, 1), (-1, -1), (-1, 1), (1, -1), (1, 1))
F32 = jnp.float32
BF16 = jnp.bfloat16


def contract(left, right, at_left, at_right):
    return lax.dot_general(
        left, right, (((at_left,), (at_right,)), ((), ())), preferred_element_type=F32
    )


def split(value):
    high = value.astype(BF16)
    return high, (value - high.astype(F32)).astype(BF16)


def remote(source, target, send, recv, row, col):
    return pltpu.make_async_remote_copy(
        src_ref=source,
        dst_ref=target,
        send_sem=send,
        recv_sem=recv,
        device_id=(row, col),
        device_id_type=MESH,
    )


def block_kernel(rows_n, cols_n, names, *refs):
    r = dict(zip(names, refs, strict=True))
    image, grad_out, taps = r["image"], r["grad_out"], r["taps"]
    pad1, pad2 = r["pad1"], r["pad2"]
    hidden, query, dout = r["hidden"], r["query"], r["dout"]
    attended, grad_query = r["attended"], r["grad_query"]
    height, width, channels = image.shape
    own = (height // POOL) * (width // POOL)
    per_row = width // POOL
    cells_n = cols_n * own
    shard = r["terms"].shape[4]
    row, col = lax.axis_index("row"), lax.axis_index("col")
    chip, core = col // 2, lax.rem(col, 2)
    chips, items = cols_n // 2, cols_n // 4
    half = items // 2
    is_cells = jnp.logical_and(chip >= half, chip < chips - half)
    is_terms = jnp.logical_or(chip < half, chip >= chips - half)

    def row_mate(step):
        return lax.rem(row + step, rows_n)

    def col_mate(step):
        return lax.rem(col + step, cols_n)

    def present(down, right):
        ok = None
        for move, at, count in ((down, row, rows_n), (right, col, cols_n)):
            if move == 0:
                continue
            here = at > 0 if move < 0 else at < count - 1
            ok = here if ok is None else jnp.logical_and(ok, here)
        return ok

    for pad in (pad1, pad2):
        for at in (0, height + 1):
            pad[at] = jnp.zeros_like(pad[at])
    for name in ("edges_in1", "edges_in2"):
        r[name][...] = jnp.zeros_like(r[name])

    barrier = pltpu.get_barrier_semaphore()
    greeted = cols_n + rows_n - 2
    for down, right in DIRECTIONS:
        greeted = greeted + present(down, right).astype(jnp.int32)

        @pl.when(present(down, right))
        def _(down=down, right=right):
            pl.semaphore_signal(barrier, inc=1, device_id=(row + down, col + right), device_id_type=MESH)
    for step in range(1, cols_n):
        pl.semaphore_signal(barrier, inc=1, device_id=(row, col_mate(step)), device_id_type=MESH)
    for step in range(1, rows_n):
        pl.semaphore_signal(barrier, inc=1, device_id=(row_mate(step), col), device_id_type=MESH)

    middle = pl.ds(EDGE, width)
    near, far = pl.ds(EDGE, EDGE), pl.ds(width, EDGE)
    before, after = pl.ds(0, EDGE), pl.ds(EDGE + width, EDGE)

    def edge(number, at):
        pad, out, got = (pad1, r["edges_out1"], r["edges_in1"]) if number == 1 else (pad2, r["edges_out2"], r["edges_in2"])
        down, right = DIRECTIONS[at]
        source = 1 if down < 0 else height
        target = height + 1 if down < 0 else 0
        if down == 0:
            source_ref, target_ref = out.at[0 if right < 0 else 1], got.at[1 if right < 0 else 0]
        elif right == 0:
            source_ref, target_ref = pad.at[source, middle], pad.at[target, middle]
        elif right < 0:
            source_ref, target_ref = pad.at[source, near], pad.at[target, after]
        else:
            source_ref, target_ref = pad.at[source, far], pad.at[target, before]
        return remote(
            source_ref, target_ref, r[f"halo_send{number}"].at[at], r[f"halo_recv{number}"].at[at], row + down, col + right
        )

    def send_halo(number):
        pad, out = (pad1, r["edges_out1"]) if number == 1 else (pad2, r["edges_out2"])
        for at in range(height):
            out[0, at : at + 1] = pad[at + 1, EDGE : EDGE + 1]
            out[1, at : at + 1] = pad[at + 1, EDGE + width - 1 : EDGE + width]
        for at, (down, right) in enumerate(DIRECTIONS):
            @pl.when(present(down, right))
            def _(at=at):
                edge(number, at).start()

    def take_halo(number):
        pad, got = (pad1, r["edges_in1"]) if number == 1 else (pad2, r["edges_in2"])
        for at, (down, right) in enumerate(DIRECTIONS):
            @pl.when(present(-down, -right))
            def _(at=at):
                edge(number, at).wait_recv()

            @pl.when(present(down, right))
            def _(at=at):
                edge(number, at).wait_send()
        for at in range(height):
            pad[at + 1, EDGE - 1 : EDGE] = got[0, at : at + 1]
            pad[at + 1, EDGE + width : EDGE + width + 1] = got[1, at : at + 1]

    @pl.loop(0, height)
    def _(at):
        pad1[at + 1, middle] = image[at].astype(F32)

    pl.semaphore_wait(barrier, greeted)
    send_halo(1)

    tokens = height * width
    chunk = tokens // 2

    @pl.loop(0, 2)
    def _(at):
        rows = pl.ds(pl.multiple_of(at * chunk, chunk), chunk)
        dout[rows] = contract(grad_out[rows], r["w_out"][...], 1, 1).astype(BF16)

    take_halo(1)

    @pl.loop(0, channels // LANES)
    def _(part):
        lanes = pl.ds(pl.multiple_of(part * LANES, LANES), LANES)
        weight = [jnp.broadcast_to(taps[i : i + 1, lanes], (width, LANES)) for i in range(9)]
        for cell_row in range(height // POOL):
            pooled = jnp.zeros((width, LANES), F32)
            for at in range(cell_row * POOL, (cell_row + 1) * POOL):
                total = jnp.zeros((width, LANES), F32)
                for i in range(9):
                    total = total + weight[i] * pad1[at + i // 3, pl.ds(EDGE - 1 + i % 3, width), lanes]
                value = (pad1[at + 1, middle, lanes] + total).astype(BF16)
                hidden[at * width : (at + 1) * width, lanes] = value
                pooled = pooled + value.astype(F32)
            r["pooled"][cell_row * per_row : (cell_row + 1) * per_row, lanes] = (
                pooled.reshape(per_row, POOL, LANES).sum(axis=1) / (POOL * POOL)
            )

    pooled = r["pooled"][...]
    centre = jnp.mean(pooled, axis=-1, keepdims=True)
    spread = jnp.mean(jnp.square(pooled - centre), axis=-1, keepdims=True)
    inverse = lax.rsqrt(spread + EPSILON)
    standard = (pooled - centre) * inverse
    cellbuf = r["cellbuf"]
    cellbuf[col] = standard.astype(BF16).astype(F32)

    def cell(step):
        return remote(
            cellbuf.at[col], cellbuf.at[col], r["cell_send"].at[step - 1], r["cell_recv"].at[step - 1], row, col_mate(step)
        )

    for step in range(1, cols_n):
        cell(step).start()

    @pl.loop(0, 2)
    def _(at):
        rows = pl.ds(pl.multiple_of(at * chunk, chunk), chunk)
        query[rows] = contract(hidden[rows], r["w_query"][...], 1, 0).astype(BF16)

    for step in range(1, cols_n):
        cell(step).wait()
    key_cells = cellbuf[...].reshape(cells_n, channels).astype(BF16)
    r["key_all"][row] = key_cells
    r["keys"][...] = contract(key_cells, r["w_key"][...], 1, 0).astype(BF16)
    r["values"][...] = contract(key_cells, r["w_value"][...], 1, 0).astype(BF16)

    pair_cells = 2 * cells_n
    same_head = (
        lax.broadcasted_iota(jnp.int32, (pair_cells, LANES), 0) // cells_n
        == lax.broadcasted_iota(jnp.int32, (pair_cells, LANES), 1) // HD
    )
    cell_ones = (
        lax.broadcasted_iota(jnp.int32, (pair_cells, pair_cells), 0) // cells_n
        == lax.broadcasted_iota(jnp.int32, (pair_cells, pair_cells), 1) // cells_n
    ).astype(F32).astype(BF16)
    lane_ones = (
        lax.broadcasted_iota(jnp.int32, (LANES, pair_cells), 0) // HD
        == lax.broadcasted_iota(jnp.int32, (LANES, pair_cells), 1) // cells_n
    ).astype(F32).astype(BF16)
    first_head = lax.broadcasted_iota(jnp.int32, (cells_n, LANES), 1) < HD
    scale = HD ** (-0.5)

    def summed(value, ones):
        high, low = split(value)
        return contract(high, ones, 1, 0) + contract(low, ones, 1, 0)

    @pl.loop(0, channels // LANES)
    def _(part):
        lanes = pl.ds(pl.multiple_of(part * LANES, LANES), LANES)

        def both(ref):
            value = ref[:, lanes].astype(F32)
            twice = jnp.concatenate([value, value], axis=0)
            return jnp.where(same_head, twice, 0.0).astype(BF16)

        key_pair, value_pair = both(r["keys"]), both(r["values"])
        queries, douts = query[:, lanes], dout[:, lanes]
        expons = jnp.exp(contract(queries, key_pair, 1, 1) * scale)
        probabilities = expons / summed(expons, cell_ones)
        weights = probabilities.astype(BF16)
        got = contract(weights, value_pair, 1, 0).astype(BF16)
        attended[:, lanes] = got
        grad_probs = contract(douts, value_pair, 1, 1)
        deltas = summed(douts.astype(F32) * got.astype(F32), lane_ones)
        grad_scores = (probabilities * (grad_probs - deltas) * scale).astype(BF16)
        grad_query[:, lanes] = contract(grad_scores, key_pair, 1, 0).astype(BF16)
        grad_key = contract(grad_scores, queries, 0, 0)
        grad_value = contract(weights, douts, 0, 0)
        grad_key = jnp.where(first_head, grad_key[:cells_n], grad_key[cells_n:])
        grad_value = jnp.where(first_head, grad_value[:cells_n], grad_value[cells_n:])
        for owner in range(cols_n):
            rows = slice(owner * own, (owner + 1) * own)
            r["blocks"][owner, :, lanes] = jnp.concatenate([grad_key[rows], grad_value[rows]], axis=0).astype(BF16)

    def block(step):
        owner = col_mate(step)
        return remote(
            r["blocks"].at[owner], r["blocks_in"].at[step - 1], r["block_send"].at[step - 1], r["block_recv"].at[step - 1], row, owner
        )

    for step in range(1, cols_n):
        block(step).start()

    terms, landed1, held1 = r["terms"], r["landed1"], r["held1"]
    landed2, held2, landed3, summed_all = r["landed2"], r["held2"], r["landed3"], r["summed_all"]

    def first(item):
        return remote(
            terms.at[1 - core, item], landed1.at[item], r["send1"].at[item], r["recv1"].at[item], row, 2 * chip + 1 - core
        )

    def second(item, step):
        return remote(
            held1.at[item, row_mate(step)], landed2.at[item, step - 1], r["send2"].at[item, step - 1],
            r["recv2"].at[item, step - 1], row_mate(step), col,
        )

    def owner_of(item):
        return item if item < half else chips - items + item

    def third(item):
        return remote(
            held2.at[item], landed3.at[chip], r["send3"].at[item], r["recv3"].at[chip], row, 2 * owner_of(item) + core
        )

    def fourth(step):
        return remote(
            summed_all.at[row], summed_all.at[row], r["send4"].at[step - 1], r["recv4"].at[step - 1], row_mate(step), col
        )

    for left, right, begin in ((hidden, grad_query, 0), (attended, grad_out, half)):
        for item in range(half):
            for side in range(2):
                at = (2 * item + side) * shard
                term = contract(left[...], right[:, at : at + shard], 0, 0).astype(BF16)
                terms[side, begin + item] = term.reshape(terms.shape[2:])
            first(begin + item).start()

    @pl.loop(0, 2)
    def _(at):
        rows = pl.ds(pl.multiple_of(at * chunk, chunk), chunk)
        value = contract(grad_query[rows], r["w_query"][...], 1, 1) + grad_out[rows].astype(F32)
        pad2[pl.ds(1 + at * (height // 2), height // 2), middle] = value.reshape(height // 2, width, channels)

    totals = r["blocks"][col].astype(F32)
    for step in range(1, cols_n):
        block(step).wait()
        totals = totals + r["blocks_in"][step - 1].astype(F32)
    high, low = split(totals)
    tot_all = r["tot_all"]
    tot_all[col] = high

    def tot(step):
        return remote(
            tot_all.at[col], tot_all.at[col], r["tot_send"].at[step - 1], r["tot_recv"].at[step - 1], row, col_mate(step)
        )

    for step in range(1, cols_n):
        tot(step).start()

    both_parts = jnp.concatenate([high, low], axis=0)
    by_key = contract(both_parts, r["w_key"][...], 1, 1)
    by_value = contract(both_parts, r["w_value"][...], 1, 1)
    grad_normed = by_key[:own] + by_key[2 * own : 3 * own] + by_value[own : 2 * own] + by_value[3 * own :]
    grad_pooled = (
        grad_normed
        - jnp.mean(grad_normed, axis=-1, keepdims=True)
        - standard * jnp.mean(grad_normed * standard, axis=-1, keepdims=True)
    ) * inverse
    grad_pooled = grad_pooled / (POOL * POOL)
    for cell_row in range(height // POOL):
        rows = grad_pooled[cell_row * per_row : (cell_row + 1) * per_row]
        over = jnp.broadcast_to(rows[:, None, :], (per_row, POOL, channels)).reshape(width, channels)
        r["over"][cell_row] = over

    @pl.loop(0, height)
    def _(at):
        pad2[at + 1, middle] = pad2[at + 1, middle] + r["over"][at // POOL]

    send_halo(2)

    for item in range(items):
        first(item).wait_recv()
        for step in range(1, rows_n + 1):
            there = row_mate(step)
            held1[item, there] = (
                terms[core, item, there].astype(F32) + landed1[item, there].astype(F32)
            ).astype(BF16)
            if step < rows_n:
                second(item, step).start()

    r["tap_terms"][...] = jnp.zeros_like(r["tap_terms"])

    @pl.loop(0, channels // LANES)
    def _(part):
        lanes = pl.ds(pl.multiple_of(part * LANES, LANES), LANES)
        sums = [jnp.zeros((8, LANES), F32) for _ in range(9)]
        for at in range(height):
            value = pad2[at + 1, middle, lanes]
            for i in range(9):
                product = value * pad1[at + i // 3, pl.ds(EDGE - 1 + i % 3, width), lanes]
                sums[i] = sums[i] + product.reshape(width // 8, 8, LANES).sum(axis=0)
        for i in range(9):
            r["tap_terms"][i : i + 1, lanes] = sums[i].sum(axis=0, keepdims=True)

    tap_out, tap_in, tap_out2, tap_in2 = r["tap_out"], r["tap_in"], r["tap_out2"], r["tap_in2"]
    tap_out[...] = r["tap_terms"][...].astype(BF16)

    def tap_first(step):
        return remote(tap_out, tap_in.at[step - 1], r["tap_send1"].at[step - 1], r["tap_recv1"].at[step - 1], row_mate(step), col)

    def tap_second(step):
        return remote(tap_out2, tap_in2.at[step - 1], r["tap_send2"].at[step - 1], r["tap_recv2"].at[step - 1], row, col_mate(step))

    for step in range(1, rows_n):
        tap_first(step).start()

    for item in range(items):
        total = held1[item, row].astype(F32)
        for step in range(1, rows_n):
            second(item, step).wait_recv()
            total = total + landed2[item, step - 1].astype(F32)
        held2[item] = total.astype(BF16)

        @pl.when(chip != owner_of(item))
        def _(item=item):
            third(item).start()

    for step in range(1, cols_n):
        tot(step).wait()
    is_key = col < 2 * items
    sides = []
    for at in range(cols_n):
        value = tot_all[at].astype(F32)
        sides.append(jnp.where(is_key, value[:own], value[own:]))
    r["side_all"][row] = jnp.concatenate(sides, axis=0).astype(BF16)

    def pass_on(name, step):
        return remote(
            r[name].at[row], r[name].at[row], r[name + "_send"].at[step - 1], r[name + "_recv"].at[step - 1], row_mate(step), col
        )

    @pl.when(is_cells)
    def _():
        for name in ("key_all", "side_all"):
            for step in range(1, rows_n):
                pass_on(name, step).start()

    tap_total = tap_out[...].astype(F32)
    for step in range(1, rows_n):
        tap_first(step).wait()
        tap_total = tap_total + tap_in[step - 1].astype(F32)
    tap_out2[...] = tap_total.astype(BF16)
    for step in range(1, cols_n):
        tap_second(step).start()

    take_halo(2)

    @pl.loop(0, channels // LANES)
    def _(part):
        lanes = pl.ds(pl.multiple_of(part * LANES, LANES), LANES)
        weight = [jnp.broadcast_to(taps[i : i + 1, lanes], (width, LANES)) for i in range(9)]
        for at in range(height):
            total = pad2[at + 1, middle, lanes]
            for i in range(9):
                total = total + weight[i] * pad2[at + 2 - i // 3, pl.ds(EDGE + 1 - i % 3, width), lanes]
            r["grad_image"][at, :, lanes] = total.astype(BF16)

    @pl.when(is_terms)
    def _():
        mine = lax.rem(chip, chips - items)
        total = held2[mine].astype(F32)
        for step in range(1, chips):
            source = lax.rem(chip + step, chips)
            remote(
                held2.at[0], landed3.at[source], r["send3"].at[0], r["recv3"].at[source], row, 2 * source + core
            ).wait_recv()
            total = total + landed3[source].astype(F32)
        summed_all[row] = total.astype(BF16)
        for step in range(1, rows_n):
            fourth(step).start()

    tap_total = tap_out2[...].astype(F32)
    for step in range(1, cols_n):
        tap_second(step).wait()
        tap_total = tap_total + tap_in2[step - 1].astype(F32)
    r["tap_sum"][...] = tap_total

    for item in range(items):
        first(item).wait_send()
        for step in range(1, rows_n):
            second(item, step).wait_send()

        @pl.when(chip != owner_of(item))
        def _(item=item):
            third(item).wait_send()

    @pl.when(is_terms)
    def _():
        for step in range(1, rows_n):
            fourth(step).wait()

    @pl.when(is_cells)
    def _():
        for name in ("key_all", "side_all"):
            for step in range(1, rows_n):
                pass_on(name, step).wait()


def on_device(image, conv_taps, w_query, w_key, w_value, w_out, grad_out):
    rows_n, cols_n = lax.axis_size("row"), lax.axis_size("col")
    height, width, channels = image.shape
    tokens = height * width
    own = (height // POOL) * (width // POOL)
    cells_n = cols_n * own
    chips, items = cols_n // 2, cols_n // 4
    shard = 4 * channels // cols_n
    high = channels // rows_n
    operands = dict(
        image=image, grad_out=grad_out.reshape(tokens, channels), taps=conv_taps,
        w_query=w_query, w_key=w_key, w_value=w_value, w_out=w_out,
    )
    shapes = dict(
        grad_image=(image.shape, BF16),
        summed_all=((rows_n, high, shard), BF16),
        key_all=((rows_n, cells_n, channels), BF16),
        side_all=((rows_n, cells_n, channels), BF16),
        tap_sum=((16, channels), F32),
    )
    scratch = dict(
        pad1=((height + 2, width + 2 * EDGE, channels), F32),
        pad2=((height + 2, width + 2 * EDGE, channels), F32),
        edges_out1=((2, height, channels), F32), edges_in1=((2, height, channels), F32),
        edges_out2=((2, height, channels), F32), edges_in2=((2, height, channels), F32),
        hidden=((tokens, channels), BF16), query=((tokens, channels), BF16), dout=((tokens, channels), BF16),
        attended=((tokens, channels), BF16), grad_query=((tokens, channels), BF16),
        pooled=((own, channels), F32), over=((height // POOL, width, channels), F32),
        cellbuf=((cols_n, own, channels), F32),
        keys=((cells_n, channels), BF16), values=((cells_n, channels), BF16),
        blocks=((cols_n, 2 * own, channels), BF16), blocks_in=((cols_n - 1, 2 * own, channels), BF16),
        tot_all=((cols_n, 2 * own, channels), BF16),
        terms=((2, items, rows_n, high, shard), BF16),
        landed1=((items, rows_n, high, shard), BF16), held1=((items, rows_n, high, shard), BF16),
        landed2=((items, rows_n - 1, high, shard), BF16), held2=((items, high, shard), BF16),
        landed3=((chips, high, shard), BF16),
        tap_terms=((16, channels), F32),
        tap_out=((16, channels), BF16), tap_in=((rows_n - 1, 16, channels), BF16),
        tap_out2=((16, channels), BF16), tap_in2=((cols_n - 1, 16, channels), BF16),
    )
    sems = dict(
        halo_send1=(8,), halo_recv1=(8,), halo_send2=(8,), halo_recv2=(8,),
        cell_send=(cols_n - 1,), cell_recv=(cols_n - 1,),
        block_send=(cols_n - 1,), block_recv=(cols_n - 1,),
        tot_send=(cols_n - 1,), tot_recv=(cols_n - 1,),
        send1=(items,), recv1=(items,), send2=(items, rows_n - 1), recv2=(items, rows_n - 1),
        send3=(items,), recv3=(chips,), send4=(rows_n - 1,), recv4=(rows_n - 1,),
        tap_send1=(rows_n - 1,), tap_recv1=(rows_n - 1,),
        tap_send2=(cols_n - 1,), tap_recv2=(cols_n - 1,),
        key_all_send=(rows_n - 1,), key_all_recv=(rows_n - 1,),
        side_all_send=(rows_n - 1,), side_all_recv=(rows_n - 1,),
    )
    names = list(operands) + list(shapes) + list(scratch) + list(sems)
    grad_image, summed_all, key_all, side_all, tap_sum = pl.pallas_call(
        partial(block_kernel, rows_n, cols_n, names),
        out_shape=[jax.ShapeDtypeStruct(*spec) for spec in shapes.values()],
        in_specs=[VMEM] * len(operands),
        out_specs=[VMEM] * len(shapes),
        scratch_shapes=[pltpu.VMEM(*spec) for spec in scratch.values()]
        + [pltpu.SemaphoreType.DMA(spec) for spec in sems.values()],
        compiler_params=pltpu.CompilerParams(
            collective_id=0, has_side_effects=True, vmem_limit_bytes=60 * 2**20
        ),
    )(*operands.values())
    quarter = cols_n // 4
    col = lax.axis_index("col")
    mine = lax.dynamic_slice_in_dim(
        side_all.reshape(-1, channels), lax.rem(col, quarter) * shard, shard, axis=1
    )
    from_cells = contract(key_all.reshape(-1, channels), mine, 0, 0)
    is_cells = jnp.logical_and(col >= quarter, col < cols_n - quarter)
    grad_weights = jnp.where(is_cells, from_cells, summed_all.reshape(channels, shard).astype(F32))
    grad_conv = lax.dynamic_slice_in_dim(
        tap_sum[:9], col * (channels // cols_n), channels // cols_n, axis=1
    )
    return (grad_image, grad_weights, grad_conv)


def solution(mesh):
    return jax.shard_map(
        on_device,
        mesh=mesh,
        in_specs=(P("row", "col", None), P(), P(), P(), P(), P(), P("row", "col", None)),
        out_specs=(P("row", "col", None), P(None, "col"), P(None, "col")),
        check_vma=False,
    )
```

```python
from functools import partial

import jax
import jax.numpy as jnp
from jax import lax
from jax.experimental import pallas as pl
from jax.experimental.pallas import tpu as pltpu
from jax.sharding import PartitionSpec as P

HD = 64
POOL = 8
LANES = 128
EDGE = 8

EPSILON = 1e-05
MESH = pl.DeviceIdType.MESH
VMEM = pl.BlockSpec(memory_space=pltpu.VMEM)
DIRECTIONS = ((-1, 0), (1, 0), (0, -1), (0, 1), (-1, -1), (-1, 1), (1, -1), (1, 1))
F32 = jnp.float32
BF16 = jnp.bfloat16


def contract(left, right, at_left, at_right):
    return lax.dot_general(
        left, right, (((at_left,), (at_right,)), ((), ())), preferred_element_type=F32
    )


def split(value):
    high = value.astype(BF16)
    return high, (value - high.astype(F32)).astype(BF16)


def remote(source, target, send, recv, row, col):
    return pltpu.make_async_remote_copy(
        src_ref=source,
        dst_ref=target,
        send_sem=send,
        recv_sem=recv,
        device_id=(row, col),
        device_id_type=MESH,
    )


def block_kernel(rows_n, cols_n, names, *refs):
    r = dict(zip(names, refs, strict=True))
    image, grad_out, taps = r["image"], r["grad_out"], r["taps"]
    pad1, pad2 = r["pad1"], r["pad2"]
    hidden, query, dout = r["hidden"], r["query"], r["dout"]
    attended, grad_query = r["attended"], r["grad_query"]
    height, width, channels = image.shape
    own = (height // POOL) * (width // POOL)
    per_row = width // POOL
    cells_n = cols_n * own
    shard = r["terms"].shape[4]
    row, col = lax.axis_index("row"), lax.axis_index("col")
    chip, core = col // 2, lax.rem(col, 2)
    chips, items = cols_n // 2, cols_n // 4
    half = items // 2
    is_cells = jnp.logical_and(chip >= half, chip < chips - half)
    is_terms = jnp.logical_or(chip < half, chip >= chips - half)

    def row_mate(step):
        return lax.rem(row + step, rows_n)

    def col_mate(step):
        return lax.rem(col + step, cols_n)

    def present(down, right):
        ok = None
        for move, at, count in ((down, row, rows_n), (right, col, cols_n)):
            if move == 0:
                continue
            here = at > 0 if move < 0 else at < count - 1
            ok = here if ok is None else jnp.logical_and(ok, here)
        return ok

    for pad in (pad1, pad2):
        for at in (0, height + 1):
            pad[at] = jnp.zeros_like(pad[at])
    for name in ("edges_in1", "edges_in2"):
        r[name][...] = jnp.zeros_like(r[name])

    barrier = pltpu.get_barrier_semaphore()
    greeted = cols_n + rows_n - 2
    for down, right in DIRECTIONS:
        greeted = greeted + present(down, right).astype(jnp.int32)

        @pl.when(present(down, right))
        def _(down=down, right=right):
            pl.semaphore_signal(barrier, inc=1, device_id=(row + down, col + right), device_id_type=MESH)
    for step in range(1, cols_n):
        pl.semaphore_signal(barrier, inc=1, device_id=(row, col_mate(step)), device_id_type=MESH)
    for step in range(1, rows_n):
        pl.semaphore_signal(barrier, inc=1, device_id=(row_mate(step), col), device_id_type=MESH)

    middle = pl.ds(EDGE, width)
    near, far = pl.ds(EDGE, EDGE), pl.ds(width, EDGE)
    before, after = pl.ds(0, EDGE), pl.ds(EDGE + width, EDGE)

    def edge(number, at):
        pad, out, got = (pad1, r["edges_out1"], r["edges_in1"]) if number == 1 else (pad2, r["edges_out2"], r["edges_in2"])
        down, right = DIRECTIONS[at]
        source = 1 if down < 0 else height
        target = height + 1 if down < 0 else 0
        if down == 0:
            source_ref, target_ref = out.at[0 if right < 0 else 1], got.at[1 if right < 0 else 0]
        elif right == 0:
            source_ref, target_ref = pad.at[source, middle], pad.at[target, middle]
        elif right < 0:
            source_ref, target_ref = pad.at[source, near], pad.at[target, after]
        else:
            source_ref, target_ref = pad.at[source, far], pad.at[target, before]
        return remote(
            source_ref, target_ref, r[f"halo_send{number}"].at[at], r[f"halo_recv{number}"].at[at], row + down, col + right
        )

    def send_halo(number):
        pad, out = (pad1, r["edges_out1"]) if number == 1 else (pad2, r["edges_out2"])
        for at in range(height):
            out[0, at : at + 1] = pad[at + 1, EDGE : EDGE + 1]
            out[1, at : at + 1] = pad[at + 1, EDGE + width - 1 : EDGE + width]
        for at, (down, right) in enumerate(DIRECTIONS):
            @pl.when(present(down, right))
            def _(at=at):
                edge(number, at).start()

    def take_halo(number):
        pad, got = (pad1, r["edges_in1"]) if number == 1 else (pad2, r["edges_in2"])
        for at, (down, right) in enumerate(DIRECTIONS):
            @pl.when(present(-down, -right))
            def _(at=at):
                edge(number, at).wait_recv()

            @pl.when(present(down, right))
            def _(at=at):
                edge(number, at).wait_send()
        for at in range(height):
            pad[at + 1, EDGE - 1 : EDGE] = got[0, at : at + 1]
            pad[at + 1, EDGE + width : EDGE + width + 1] = got[1, at : at + 1]

    @pl.loop(0, height)
    def _(at):
        pad1[at + 1, middle] = image[at].astype(F32)

    pl.semaphore_wait(barrier, greeted)
    send_halo(1)

    tokens = height * width
    chunk = tokens // 2

    @pl.loop(0, 2)
    def _(at):
        rows = pl.ds(pl.multiple_of(at * chunk, chunk), chunk)
        dout[rows] = contract(grad_out[rows], r["w_out"][...], 1, 1).astype(BF16)

    take_halo(1)

    @pl.loop(0, channels // LANES)
    def _(part):
        lanes = pl.ds(pl.multiple_of(part * LANES, LANES), LANES)
        weight = [jnp.broadcast_to(taps[i : i + 1, lanes], (width, LANES)) for i in range(9)]
        for cell_row in range(height // POOL):
            pooled = jnp.zeros((width, LANES), F32)
            for at in range(cell_row * POOL, (cell_row + 1) * POOL):
                total = jnp.zeros((width, LANES), F32)
                for i in range(9):
                    total = total + weight[i] * pad1[at + i // 3, pl.ds(EDGE - 1 + i % 3, width), lanes]
                value = (pad1[at + 1, middle, lanes] + total).astype(BF16)
                hidden[at * width : (at + 1) * width, lanes] = value
                pooled = pooled + value.astype(F32)
            r["pooled"][cell_row * per_row : (cell_row + 1) * per_row, lanes] = (
                pooled.reshape(per_row, POOL, LANES).sum(axis=1) / (POOL * POOL)
            )

    pooled = r["pooled"][...]
    centre = jnp.mean(pooled, axis=-1, keepdims=True)
    spread = jnp.mean(jnp.square(pooled - centre), axis=-1, keepdims=True)
    inverse = lax.rsqrt(spread + EPSILON)
    standard = (pooled - centre) * inverse
    cellbuf = r["cellbuf"]
    cellbuf[col] = standard.astype(BF16).astype(F32)

    def cell(step):
        return remote(
            cellbuf.at[col], cellbuf.at[col], r["cell_send"].at[step - 1], r["cell_recv"].at[step - 1], row, col_mate(step)
        )

    for step in range(1, cols_n):
        cell(step).start()

    @pl.loop(0, 2)
    def _(at):
        rows = pl.ds(pl.multiple_of(at * chunk, chunk), chunk)
        query[rows] = contract(hidden[rows], r["w_query"][...], 1, 0).astype(BF16)

    for step in range(1, cols_n):
        cell(step).wait()
    key_cells = cellbuf[...].reshape(cells_n, channels).astype(BF16)
    r["key_all"][row] = key_cells
    r["keys"][...] = contract(key_cells, r["w_key"][...], 1, 0).astype(BF16)
    r["values"][...] = contract(key_cells, r["w_value"][...], 1, 0).astype(BF16)

    pair_cells = 2 * cells_n
    same_head = (
        lax.broadcasted_iota(jnp.int32, (pair_cells, LANES), 0) // cells_n
        == lax.broadcasted_iota(jnp.int32, (pair_cells, LANES), 1) // HD
    )
    cell_ones = (
        lax.broadcasted_iota(jnp.int32, (pair_cells, pair_cells), 0) // cells_n
        == lax.broadcasted_iota(jnp.int32, (pair_cells, pair_cells), 1) // cells_n
    ).astype(F32).astype(BF16)
    lane_ones = (
        lax.broadcasted_iota(jnp.int32, (LANES, pair_cells), 0) // HD
        == lax.broadcasted_iota(jnp.int32, (LANES, pair_cells), 1) // cells_n
    ).astype(F32).astype(BF16)
    first_head = lax.broadcasted_iota(jnp.int32, (cells_n, LANES), 1) < HD
    scale = HD ** (-0.5)

    def summed(value, ones):
        high, low = split(value)
        return contract(high, ones, 1, 0) + contract(low, ones, 1, 0)

    @pl.loop(0, channels // LANES)
    def _(part):
        lanes = pl.ds(pl.multiple_of(part * LANES, LANES), LANES)

        def both(ref):
            value = ref[:, lanes].astype(F32)
            twice = jnp.concatenate([value, value], axis=0)
            return jnp.where(same_head, twice, 0.0).astype(BF16)

        key_pair, value_pair = both(r["keys"]), both(r["values"])
        queries, douts = query[:, lanes], dout[:, lanes]
        expons = jnp.exp(contract(queries, key_pair, 1, 1) * scale)
        probabilities = expons / summed(expons, cell_ones)
        weights = probabilities.astype(BF16)
        got = contract(weights, value_pair, 1, 0).astype(BF16)
        attended[:, lanes] = got
        grad_probs = contract(douts, value_pair, 1, 1)
        deltas = summed(douts.astype(F32) * got.astype(F32), lane_ones)
        grad_scores = (probabilities * (grad_probs - deltas) * scale).astype(BF16)
        grad_query[:, lanes] = contract(grad_scores, key_pair, 1, 0).astype(BF16)
        grad_key = contract(grad_scores, queries, 0, 0)
        grad_value = contract(weights, douts, 0, 0)
        grad_key = jnp.where(first_head, grad_key[:cells_n], grad_key[cells_n:])
        grad_value = jnp.where(first_head, grad_value[:cells_n], grad_value[cells_n:])
        for owner in range(cols_n):
            rows = slice(owner * own, (owner + 1) * own)
            r["blocks"][owner, :, lanes] = jnp.concatenate([grad_key[rows], grad_value[rows]], axis=0).astype(BF16)

    def block(step):
        owner = col_mate(step)
        return remote(
            r["blocks"].at[owner], r["blocks_in"].at[step - 1], r["block_send"].at[step - 1], r["block_recv"].at[step - 1], row, owner
        )

    for step in range(1, cols_n):
        block(step).start()

    terms, landed1, held1 = r["terms"], r["landed1"], r["held1"]
    landed2, held2, landed3, summed_all = r["landed2"], r["held2"], r["landed3"], r["summed_all"]

    def first(item):
        return remote(
            terms.at[1 - core, item], landed1.at[item], r["send1"].at[item], r["recv1"].at[item], row, 2 * chip + 1 - core
        )

    deep = terms.shape[3] // 2
    part_of = [pl.ds(sub * deep, deep) for sub in range(2)]

    def second(item, step, sub):
        return remote(
            held1.at[item, row_mate(step), part_of[sub]], landed2.at[item, step - 1, part_of[sub]],
            r["send2"].at[item, step - 1, sub], r["recv2"].at[item, step - 1, sub], row_mate(step), col,
        )

    def owner_of(item):
        return item if item < half else chips - items + item

    def third(item, sub):
        return remote(
            held2.at[item, part_of[sub]], landed3.at[chip, part_of[sub]], r["send3"].at[item, sub],
            r["recv3"].at[chip, sub], row, 2 * owner_of(item) + core,
        )

    def fourth(step, sub):
        return remote(
            summed_all.at[row, part_of[sub]], summed_all.at[row, part_of[sub]], r["send4"].at[step - 1, sub],
            r["recv4"].at[step - 1, sub], row_mate(step), col,
        )

    def start_second():
        for sub in range(2):
            for item in range(items):
                if sub == 0:
                    first(item).wait_recv()
                for step in range(1, rows_n + 1):
                    there = row_mate(step)
                    held1[item, there, part_of[sub]] = (
                        terms[core, item, there, part_of[sub]].astype(F32)
                        + landed1[item, there, part_of[sub]].astype(F32)
                    ).astype(BF16)
                    if step < rows_n:
                        second(item, step, sub).start()

    def start_third(sub):
        for item in range(items):
            total = held1[item, row, part_of[sub]].astype(F32)
            for step in range(1, rows_n):
                second(item, step, sub).wait_recv()
                total = total + landed2[item, step - 1, part_of[sub]].astype(F32)
            held2[item, part_of[sub]] = total.astype(BF16)

            @pl.when(chip != owner_of(item))
            def _(item=item):
                third(item, sub).start()

    def start_fourth(sub):
        @pl.when(is_terms)
        def _():
            mine = lax.rem(chip, chips - items)
            total = held2[mine, part_of[sub]].astype(F32)
            for step in range(1, chips):
                source = lax.rem(chip + step, chips)
                remote(
                    held2.at[0, part_of[sub]], landed3.at[source, part_of[sub]], r["send3"].at[0, sub],
                    r["recv3"].at[source, sub], row, 2 * source + core,
                ).wait_recv()
                total = total + landed3[source, part_of[sub]].astype(F32)
            summed_all[row, part_of[sub]] = total.astype(BF16)
            for step in range(1, rows_n):
                fourth(step, sub).start()

    for left, right, begin in ((hidden, grad_query, 0), (attended, grad_out, half)):
        for item in range(half):
            for side in range(2):
                at = (2 * item + side) * shard
                term = contract(left[...], right[:, at : at + shard], 0, 0).astype(BF16)
                terms[side, begin + item] = term.reshape(terms.shape[2:])
            first(begin + item).start()

    @pl.loop(0, 2)
    def _(at):
        rows = pl.ds(pl.multiple_of(at * chunk, chunk), chunk)
        value = contract(grad_query[rows], r["w_query"][...], 1, 1) + grad_out[rows].astype(F32)
        pad2[pl.ds(1 + at * (height // 2), height // 2), middle] = value.reshape(height // 2, width, channels)

    start_second()

    totals = r["blocks"][col].astype(F32)
    for step in range(1, cols_n):
        block(step).wait()
        totals = totals + r["blocks_in"][step - 1].astype(F32)
    high, low = split(totals)
    tot_all = r["tot_all"]
    tot_all[col] = high

    def tot(step):
        return remote(
            tot_all.at[col], tot_all.at[col], r["tot_send"].at[step - 1], r["tot_recv"].at[step - 1], row, col_mate(step)
        )

    for step in range(1, cols_n):
        tot(step).start()

    both_parts = jnp.concatenate([high, low], axis=0)
    by_key = contract(both_parts, r["w_key"][...], 1, 1)
    by_value = contract(both_parts, r["w_value"][...], 1, 1)
    grad_normed = by_key[:own] + by_key[2 * own : 3 * own] + by_value[own : 2 * own] + by_value[3 * own :]
    grad_pooled = (
        grad_normed
        - jnp.mean(grad_normed, axis=-1, keepdims=True)
        - standard * jnp.mean(grad_normed * standard, axis=-1, keepdims=True)
    ) * inverse
    grad_pooled = grad_pooled / (POOL * POOL)
    for cell_row in range(height // POOL):
        rows = grad_pooled[cell_row * per_row : (cell_row + 1) * per_row]
        over = jnp.broadcast_to(rows[:, None, :], (per_row, POOL, channels)).reshape(width, channels)
        r["over"][cell_row] = over

    @pl.loop(0, height)
    def _(at):
        pad2[at + 1, middle] = pad2[at + 1, middle] + r["over"][at // POOL]

    send_halo(2)

    r["tap_terms"][...] = jnp.zeros_like(r["tap_terms"])

    @pl.loop(0, channels // LANES)
    def _(part):
        lanes = pl.ds(pl.multiple_of(part * LANES, LANES), LANES)
        sums = [jnp.zeros((8, LANES), F32) for _ in range(9)]
        for at in range(height):
            value = pad2[at + 1, middle, lanes]
            for i in range(9):
                product = value * pad1[at + i // 3, pl.ds(EDGE - 1 + i % 3, width), lanes]
                sums[i] = sums[i] + product.reshape(width // 8, 8, LANES).sum(axis=0)
        for i in range(9):
            r["tap_terms"][i : i + 1, lanes] = sums[i].sum(axis=0, keepdims=True)

    tap_out, tap_in, tap_out2, tap_in2 = r["tap_out"], r["tap_in"], r["tap_out2"], r["tap_in2"]
    tap_out[...] = r["tap_terms"][...].astype(BF16)

    def tap_first(step):
        return remote(tap_out, tap_in.at[step - 1], r["tap_send1"].at[step - 1], r["tap_recv1"].at[step - 1], row_mate(step), col)

    def tap_second(step):
        return remote(tap_out2, tap_in2.at[step - 1], r["tap_send2"].at[step - 1], r["tap_recv2"].at[step - 1], row, col_mate(step))

    for step in range(1, rows_n):
        tap_first(step).start()

    start_third(0)

    for step in range(1, cols_n):
        tot(step).wait()
    is_key = col < 2 * items
    sides = []
    for at in range(cols_n):
        value = tot_all[at].astype(F32)
        sides.append(jnp.where(is_key, value[:own], value[own:]))
    r["side_all"][row] = jnp.concatenate(sides, axis=0).astype(BF16)

    def pass_on(name, step):
        return remote(
            r[name].at[row], r[name].at[row], r[name + "_send"].at[step - 1], r[name + "_recv"].at[step - 1], row_mate(step), col
        )

    @pl.when(is_cells)
    def _():
        for name in ("key_all", "side_all"):
            for step in range(1, rows_n):
                pass_on(name, step).start()

    tap_total = tap_out[...].astype(F32)
    for step in range(1, rows_n):
        tap_first(step).wait()
        tap_total = tap_total + tap_in[step - 1].astype(F32)
    tap_out2[...] = tap_total.astype(BF16)
    for step in range(1, cols_n):
        tap_second(step).start()

    start_third(1)
    take_halo(2)

    @pl.loop(0, channels // LANES)
    def _(part):
        lanes = pl.ds(pl.multiple_of(part * LANES, LANES), LANES)
        weight = [jnp.broadcast_to(taps[i : i + 1, lanes], (width, LANES)) for i in range(9)]
        for at in range(height):
            total = pad2[at + 1, middle, lanes]
            for i in range(9):
                total = total + weight[i] * pad2[at + 2 - i // 3, pl.ds(EDGE + 1 - i % 3, width), lanes]
            r["grad_image"][at, :, lanes] = total.astype(BF16)

    start_fourth(0)
    start_fourth(1)

    tap_total = tap_out2[...].astype(F32)
    for step in range(1, cols_n):
        tap_second(step).wait()
        tap_total = tap_total + tap_in2[step - 1].astype(F32)
    r["tap_sum"][...] = tap_total

    for item in range(items):
        first(item).wait_send()
        for step in range(1, rows_n):
            for sub in range(2):
                second(item, step, sub).wait_send()

        @pl.when(chip != owner_of(item))
        def _(item=item):
            for sub in range(2):
                third(item, sub).wait_send()

    @pl.when(is_terms)
    def _():
        for step in range(1, rows_n):
            for sub in range(2):
                fourth(step, sub).wait()

    @pl.when(is_cells)
    def _():
        for name in ("key_all", "side_all"):
            for step in range(1, rows_n):
                pass_on(name, step).wait()


def on_device(image, conv_taps, w_query, w_key, w_value, w_out, grad_out):
    rows_n, cols_n = lax.axis_size("row"), lax.axis_size("col")
    height, width, channels = image.shape
    tokens = height * width
    own = (height // POOL) * (width // POOL)
    cells_n = cols_n * own
    chips, items = cols_n // 2, cols_n // 4
    shard = 4 * channels // cols_n
    high = channels // rows_n
    operands = dict(
        image=image, grad_out=grad_out.reshape(tokens, channels), taps=conv_taps,
        w_query=w_query, w_key=w_key, w_value=w_value, w_out=w_out,
    )
    shapes = dict(
        grad_image=(image.shape, BF16),
        summed_all=((rows_n, high, shard), BF16),
        key_all=((rows_n, cells_n, channels), BF16),
        side_all=((rows_n, cells_n, channels), BF16),
        tap_sum=((16, channels), F32),
    )
    scratch = dict(
        pad1=((height + 2, width + 2 * EDGE, channels), F32),
        pad2=((height + 2, width + 2 * EDGE, channels), F32),
        edges_out1=((2, height, channels), F32), edges_in1=((2, height, channels), F32),
        edges_out2=((2, height, channels), F32), edges_in2=((2, height, channels), F32),
        hidden=((tokens, channels), BF16), query=((tokens, channels), BF16), dout=((tokens, channels), BF16),
        attended=((tokens, channels), BF16), grad_query=((tokens, channels), BF16),
        pooled=((own, channels), F32), over=((height // POOL, width, channels), F32),
        cellbuf=((cols_n, own, channels), F32),
        keys=((cells_n, channels), BF16), values=((cells_n, channels), BF16),
        blocks=((cols_n, 2 * own, channels), BF16), blocks_in=((cols_n - 1, 2 * own, channels), BF16),
        tot_all=((cols_n, 2 * own, channels), BF16),
        terms=((2, items, rows_n, high, shard), BF16),
        landed1=((items, rows_n, high, shard), BF16), held1=((items, rows_n, high, shard), BF16),
        landed2=((items, rows_n - 1, high, shard), BF16), held2=((items, high, shard), BF16),
        landed3=((chips, high, shard), BF16),
        tap_terms=((16, channels), F32),
        tap_out=((16, channels), BF16), tap_in=((rows_n - 1, 16, channels), BF16),
        tap_out2=((16, channels), BF16), tap_in2=((cols_n - 1, 16, channels), BF16),
    )
    sems = dict(
        halo_send1=(8,), halo_recv1=(8,), halo_send2=(8,), halo_recv2=(8,),
        cell_send=(cols_n - 1,), cell_recv=(cols_n - 1,),
        block_send=(cols_n - 1,), block_recv=(cols_n - 1,),
        tot_send=(cols_n - 1,), tot_recv=(cols_n - 1,),
        send1=(items,), recv1=(items,), send2=(items, rows_n - 1, 2), recv2=(items, rows_n - 1, 2),
        send3=(items, 2), recv3=(chips, 2), send4=(rows_n - 1, 2), recv4=(rows_n - 1, 2),
        tap_send1=(rows_n - 1,), tap_recv1=(rows_n - 1,),
        tap_send2=(cols_n - 1,), tap_recv2=(cols_n - 1,),
        key_all_send=(rows_n - 1,), key_all_recv=(rows_n - 1,),
        side_all_send=(rows_n - 1,), side_all_recv=(rows_n - 1,),
    )
    names = list(operands) + list(shapes) + list(scratch) + list(sems)
    grad_image, summed_all, key_all, side_all, tap_sum = pl.pallas_call(
        partial(block_kernel, rows_n, cols_n, names),
        out_shape=[jax.ShapeDtypeStruct(*spec) for spec in shapes.values()],
        in_specs=[VMEM] * len(operands),
        out_specs=[VMEM] * len(shapes),
        scratch_shapes=[pltpu.VMEM(*spec) for spec in scratch.values()]
        + [pltpu.SemaphoreType.DMA(spec) for spec in sems.values()],
        compiler_params=pltpu.CompilerParams(
            collective_id=0, has_side_effects=True, vmem_limit_bytes=60 * 2**20
        ),
    )(*operands.values())
    quarter = cols_n // 4
    col = lax.axis_index("col")
    mine = lax.dynamic_slice_in_dim(
        side_all.reshape(-1, channels), lax.rem(col, quarter) * shard, shard, axis=1
    )
    from_cells = contract(key_all.reshape(-1, channels), mine, 0, 0)
    is_cells = jnp.logical_and(col >= quarter, col < cols_n - quarter)
    grad_weights = jnp.where(is_cells, from_cells, summed_all.reshape(channels, shard).astype(F32))
    grad_conv = lax.dynamic_slice_in_dim(
        tap_sum[:9], col * (channels // cols_n), channels // cols_n, axis=1
    )
    return (grad_image, grad_weights, grad_conv)


def solution(mesh):
    return jax.shard_map(
        on_device,
        mesh=mesh,
        in_specs=(P("row", "col", None), P(), P(), P(), P(), P(), P("row", "col", None)),
        out_specs=(P("row", "col", None), P(None, "col"), P(None, "col")),
        check_vma=False,
    )
```

```python
from functools import partial

import jax
import jax.numpy as jnp
from jax import lax
from jax.experimental import pallas as pl
from jax.experimental.pallas import tpu as pltpu
from jax.sharding import PartitionSpec as P

HD = 64
POOL = 8
LANES = 128
EDGE = 8

EPSILON = 1e-05
MESH = pl.DeviceIdType.MESH
VMEM = pl.BlockSpec(memory_space=pltpu.VMEM)
DIRECTIONS = ((-1, 0), (1, 0), (0, -1), (0, 1), (-1, -1), (-1, 1), (1, -1), (1, 1))
F32 = jnp.float32
BF16 = jnp.bfloat16


def contract(left, right, at_left, at_right):
    return lax.dot_general(
        left, right, (((at_left,), (at_right,)), ((), ())), preferred_element_type=F32
    )


def split(value):
    high = value.astype(BF16)
    return high, (value - high.astype(F32)).astype(BF16)


def remote(source, target, send, recv, row, col):
    return pltpu.make_async_remote_copy(
        src_ref=source,
        dst_ref=target,
        send_sem=send,
        recv_sem=recv,
        device_id=(row, col),
        device_id_type=MESH,
    )


def block_kernel(rows_n, cols_n, names, *refs):
    r = dict(zip(names, refs, strict=True))
    image, grad_out, taps = r["image"], r["grad_out"], r["taps"]
    pad1, pad2 = r["pad1"], r["pad2"]
    hidden, query, dout = r["hidden"], r["query"], r["dout"]
    attended, grad_query = r["attended"], r["grad_query"]
    height, width, channels = image.shape
    own = (height // POOL) * (width // POOL)
    per_row = width // POOL
    cells_n = cols_n * own
    shard = r["terms"].shape[4]
    row, col = lax.axis_index("row"), lax.axis_index("col")
    chip, core = col // 2, lax.rem(col, 2)
    chips, items = cols_n // 2, cols_n // 4
    half = items // 2
    is_cells = jnp.logical_and(chip >= half, chip < chips - half)
    is_terms = jnp.logical_or(chip < half, chip >= chips - half)

    def row_mate(step):
        return lax.rem(row + step, rows_n)

    def col_mate(step):
        return lax.rem(col + step, cols_n)

    def present(down, right):
        ok = None
        for move, at, count in ((down, row, rows_n), (right, col, cols_n)):
            if move == 0:
                continue
            here = at > 0 if move < 0 else at < count - 1
            ok = here if ok is None else jnp.logical_and(ok, here)
        return ok

    for at in (0, height + 1):
        pad2[at] = jnp.zeros_like(pad2[at])
    for name in ("edges_in1", "edges_in2", "rows_in1", "corners_in1"):
        r[name][...] = jnp.zeros_like(r[name])

    barrier = pltpu.get_barrier_semaphore()
    greeted = cols_n + rows_n - 2
    for down, right in DIRECTIONS:
        greeted = greeted + present(down, right).astype(jnp.int32)

        @pl.when(present(down, right))
        def _(down=down, right=right):
            pl.semaphore_signal(barrier, inc=1, device_id=(row + down, col + right), device_id_type=MESH)
    for step in range(1, cols_n):
        pl.semaphore_signal(barrier, inc=1, device_id=(row, col_mate(step)), device_id_type=MESH)
    for step in range(1, rows_n):
        pl.semaphore_signal(barrier, inc=1, device_id=(row_mate(step), col), device_id_type=MESH)

    middle = pl.ds(EDGE, width)
    near, far = pl.ds(EDGE, EDGE), pl.ds(width, EDGE)
    before, after = pl.ds(0, EDGE), pl.ds(EDGE + width, EDGE)

    def edge(number, at):
        pad, out, got = (pad1, r["edges_out1"], r["edges_in1"]) if number == 1 else (pad2, r["edges_out2"], r["edges_in2"])
        down, right = DIRECTIONS[at]
        source = 1 if down < 0 else height
        target = height + 1 if down < 0 else 0
        if down == 0:
            source_ref, target_ref = out.at[0 if right < 0 else 1], got.at[1 if right < 0 else 0]
        elif number == 1 and right == 0:
            source_ref, target_ref = image.at[source - 1], r["rows_in1"].at[1 if down < 0 else 0]
        elif number == 1:
            source_ref = image.at[source - 1, pl.ds(0 if right < 0 else width - 2 * EDGE, 2 * EDGE)]
            target_ref = r["corners_in1"].at[(2 if down < 0 else 0) + (1 if right < 0 else 0)]
        elif right == 0:
            source_ref, target_ref = pad.at[source, middle], pad.at[target, middle]
        elif right < 0:
            source_ref, target_ref = pad.at[source, near], pad.at[target, after]
        else:
            source_ref, target_ref = pad.at[source, far], pad.at[target, before]
        return remote(
            source_ref, target_ref, r[f"halo_send{number}"].at[at], r[f"halo_recv{number}"].at[at], row + down, col + right
        )

    def send_halo(number):
        pad, out = (pad1, r["edges_out1"]) if number == 1 else (pad2, r["edges_out2"])
        for at in range(height):
            if number == 1:
                out[0, at : at + 1] = image[at, : 2 * EDGE].astype(F32)[:1]
                out[1, at : at + 1] = image[at, width - 2 * EDGE :].astype(F32)[2 * EDGE - 1 :]
            else:
                out[0, at : at + 1] = pad[at + 1, EDGE : EDGE + 1]
                out[1, at : at + 1] = pad[at + 1, EDGE + width - 1 : EDGE + width]
        if number == 1:
            pl.semaphore_wait(barrier, greeted)
        for at, (down, right) in enumerate(DIRECTIONS):
            @pl.when(present(down, right))
            def _(at=at):
                edge(number, at).start()

    def wait_edges(number, wanted):
        for at, (down, right) in enumerate(DIRECTIONS):
            if (down == 0) not in wanted:
                continue

            @pl.when(present(-down, -right))
            def _(at=at):
                edge(number, at).wait_recv()

            @pl.when(present(down, right))
            def _(at=at):
                edge(number, at).wait_send()

    def take_cols(number):
        pad, got = (pad1, r["edges_in1"]) if number == 1 else (pad2, r["edges_in2"])
        for at in range(height):
            pad[at + 1, EDGE - 1 : EDGE] = got[0, at : at + 1]
            pad[at + 1, EDGE + width : EDGE + width + 1] = got[1, at : at + 1]

    send_halo(1)

    @pl.loop(0, height)
    def _(at):
        pad1[at + 1, middle] = image[at].astype(F32)

    tokens = height * width
    chunk = tokens // 2

    @pl.loop(0, 2)
    def _(at):
        rows = pl.ds(pl.multiple_of(at * chunk, chunk), chunk)
        dout[rows] = contract(grad_out[rows], r["w_out"][...], 1, 1).astype(BF16)

    def mix(wanted, begin):
        @pl.loop(0, channels // LANES)
        def _(part):
            lanes = pl.ds(pl.multiple_of(part * LANES, LANES), LANES)
            weight = [jnp.broadcast_to(taps[i : i + 1, lanes], (width, LANES)) for i in range(9)]
            for cell_row in range(height // POOL):
                pooled = jnp.zeros((width, LANES), F32)
                some = False
                for at in range(cell_row * POOL, (cell_row + 1) * POOL):
                    if at not in wanted:
                        continue
                    some = True
                    total = jnp.zeros((width, LANES), F32)
                    for i in range(9):
                        total = total + weight[i] * pad1[at + i // 3, pl.ds(EDGE - 1 + i % 3, width), lanes]
                    value = (pad1[at + 1, middle, lanes] + total).astype(BF16)
                    hidden[at * width : (at + 1) * width, lanes] = value
                    pooled = pooled + value.astype(F32)
                if some:
                    where = slice(cell_row * per_row, (cell_row + 1) * per_row)
                    sums = pooled.reshape(per_row, POOL, LANES).sum(axis=1) / (POOL * POOL)
                    r["pooled"][where, lanes] = sums if begin else r["pooled"][where, lanes] + sums

    wait_edges(1, (True,))
    take_cols(1)
    mix(range(1, height - 1), True)
    wait_edges(1, (False,))
    for at, side in ((0, 0), (height + 1, 1)):
        pad1[at, middle] = r["rows_in1"][side].astype(F32)
        pad1[at, EDGE - 1 : EDGE] = r["corners_in1"][2 * side].astype(F32)[2 * EDGE - 1 :]
        pad1[at, EDGE + width : EDGE + width + 1] = r["corners_in1"][2 * side + 1].astype(F32)[:1]
    mix((0, height - 1), False)

    pooled = r["pooled"][...]
    centre = jnp.mean(pooled, axis=-1, keepdims=True)
    spread = jnp.mean(jnp.square(pooled - centre), axis=-1, keepdims=True)
    inverse = lax.rsqrt(spread + EPSILON)
    standard = (pooled - centre) * inverse
    cellbuf = r["cellbuf"]
    cellbuf[col] = standard.astype(BF16)

    def cell(step):
        return remote(
            cellbuf.at[col], cellbuf.at[col], r["cell_send"].at[step - 1], r["cell_recv"].at[step - 1], row, col_mate(step)
        )

    for step in range(1, cols_n):
        cell(step).start()

    @pl.loop(0, 2)
    def _(at):
        rows = pl.ds(pl.multiple_of(at * chunk, chunk), chunk)
        query[rows] = contract(hidden[rows], r["w_query"][...], 1, 0).astype(BF16)

    for step in range(1, cols_n):
        cell(step).wait()
    key_cells = jnp.concatenate([cellbuf[at].astype(F32) for at in range(cols_n)], axis=0).astype(BF16)
    r["key_all"][row] = key_cells
    r["keys"][...] = contract(key_cells, r["w_key"][...], 1, 0).astype(BF16)
    r["values"][...] = contract(key_cells, r["w_value"][...], 1, 0).astype(BF16)

    pair_cells = 2 * cells_n
    same_head = (
        lax.broadcasted_iota(jnp.int32, (pair_cells, LANES), 0) // cells_n
        == lax.broadcasted_iota(jnp.int32, (pair_cells, LANES), 1) // HD
    )
    cell_ones = (
        lax.broadcasted_iota(jnp.int32, (pair_cells, pair_cells), 0) // cells_n
        == lax.broadcasted_iota(jnp.int32, (pair_cells, pair_cells), 1) // cells_n
    ).astype(F32).astype(BF16)
    lane_ones = (
        lax.broadcasted_iota(jnp.int32, (LANES, pair_cells), 0) // HD
        == lax.broadcasted_iota(jnp.int32, (LANES, pair_cells), 1) // cells_n
    ).astype(F32).astype(BF16)
    first_head = lax.broadcasted_iota(jnp.int32, (cells_n, LANES), 1) < HD
    scale = HD ** (-0.5)

    def summed(value, ones):
        high, low = split(value)
        return contract(high, ones, 1, 0) + contract(low, ones, 1, 0)

    @pl.loop(0, channels // LANES)
    def _(part):
        lanes = pl.ds(pl.multiple_of(part * LANES, LANES), LANES)

        def both(ref):
            value = ref[:, lanes].astype(F32)
            twice = jnp.concatenate([value, value], axis=0)
            return jnp.where(same_head, twice, 0.0).astype(BF16)

        key_pair, value_pair = both(r["keys"]), both(r["values"])
        queries, douts = query[:, lanes], dout[:, lanes]
        expons = jnp.exp(contract(queries, key_pair, 1, 1) * scale)
        probabilities = expons / summed(expons, cell_ones)
        weights = probabilities.astype(BF16)
        got = contract(weights, value_pair, 1, 0).astype(BF16)
        attended[:, lanes] = got
        grad_probs = contract(douts, value_pair, 1, 1)
        deltas = summed(douts.astype(F32) * got.astype(F32), lane_ones)
        grad_scores = (probabilities * (grad_probs - deltas) * scale).astype(BF16)
        grad_query[:, lanes] = contract(grad_scores, key_pair, 1, 0).astype(BF16)
        grad_key = contract(grad_scores, queries, 0, 0)
        grad_value = contract(weights, douts, 0, 0)
        grad_key = jnp.where(first_head, grad_key[:cells_n], grad_key[cells_n:])
        grad_value = jnp.where(first_head, grad_value[:cells_n], grad_value[cells_n:])
        for owner in range(cols_n):
            rows = slice(owner * own, (owner + 1) * own)
            r["blocks"][owner, :, lanes] = jnp.concatenate([grad_key[rows], grad_value[rows]], axis=0).astype(BF16)

    def block(step):
        owner = col_mate(step)
        return remote(
            r["blocks"].at[owner], r["blocks_in"].at[step - 1], r["block_send"].at[step - 1], r["block_recv"].at[step - 1], row, owner
        )

    for step in range(1, cols_n):
        block(step).start()

    terms, landed1, held1 = r["terms"], r["landed1"], r["held1"]
    landed2, held2, landed3, summed_all = r["landed2"], r["held2"], r["landed3"], r["summed_all"]

    def first(item):
        return remote(
            terms.at[1 - core, item], landed1.at[item], r["send1"].at[item], r["recv1"].at[item], row, 2 * chip + 1 - core
        )

    deep = terms.shape[3] // 2
    part_of = [pl.ds(sub * deep, deep) for sub in range(2)]

    def second(item, step, sub):
        return remote(
            held1.at[item, row_mate(step), part_of[sub]], landed2.at[item, step - 1, part_of[sub]],
            r["send2"].at[item, step - 1, sub], r["recv2"].at[item, step - 1, sub], row_mate(step), col,
        )

    def owner_of(item):
        return item if item < half else chips - items + item

    def third(item, sub):
        return remote(
            held2.at[item, part_of[sub]], landed3.at[chip, part_of[sub]], r["send3"].at[item, sub],
            r["recv3"].at[chip, sub], row, 2 * owner_of(item) + core,
        )

    def fourth(step, sub):
        return remote(
            summed_all.at[row, part_of[sub]], summed_all.at[row, part_of[sub]], r["send4"].at[step - 1, sub],
            r["recv4"].at[step - 1, sub], row_mate(step), col,
        )

    def start_second():
        for sub in range(2):
            for item in range(items):
                if sub == 0:
                    first(item).wait_recv()
                for step in range(1, rows_n + 1):
                    there = row_mate(step)
                    held1[item, there, part_of[sub]] = (
                        terms[core, item, there, part_of[sub]].astype(F32)
                        + landed1[item, there, part_of[sub]].astype(F32)
                    ).astype(BF16)
                    if step < rows_n:
                        second(item, step, sub).start()

    def start_third(sub):
        for item in range(items):
            total = held1[item, row, part_of[sub]].astype(F32)
            for step in range(1, rows_n):
                second(item, step, sub).wait_recv()
                total = total + landed2[item, step - 1, part_of[sub]].astype(F32)
            held2[item, part_of[sub]] = total.astype(BF16)

            @pl.when(chip != owner_of(item))
            def _(item=item):
                third(item, sub).start()

    def start_fourth(sub):
        @pl.when(is_terms)
        def _():
            mine = lax.rem(chip, chips - items)
            total = held2[mine, part_of[sub]].astype(F32)
            for step in range(1, chips):
                source = lax.rem(chip + step, chips)
                remote(
                    held2.at[0, part_of[sub]], landed3.at[source, part_of[sub]], r["send3"].at[0, sub],
                    r["recv3"].at[source, sub], row, 2 * source + core,
                ).wait_recv()
                total = total + landed3[source, part_of[sub]].astype(F32)
            summed_all[row, part_of[sub]] = total.astype(BF16)
            for step in range(1, rows_n):
                fourth(step, sub).start()

    for left, right, begin in ((hidden, grad_query, 0), (attended, grad_out, half)):
        for item in range(half):
            for side in range(2):
                at = (2 * item + side) * shard
                term = contract(left[...], right[:, at : at + shard], 0, 0).astype(BF16)
                terms[side, begin + item] = term.reshape(terms.shape[2:])
            first(begin + item).start()

    @pl.loop(0, 2)
    def _(at):
        rows = pl.ds(pl.multiple_of(at * chunk, chunk), chunk)
        value = contract(grad_query[rows], r["w_query"][...], 1, 1) + grad_out[rows].astype(F32)
        pad2[pl.ds(1 + at * (height // 2), height // 2), middle] = value.reshape(height // 2, width, channels)

    start_second()

    totals = r["blocks"][col].astype(F32)
    for step in range(1, cols_n):
        block(step).wait()
        totals = totals + r["blocks_in"][step - 1].astype(F32)
    high, low = split(totals)
    tot_all = r["tot_all"]
    tot_all[col] = high

    def tot(step):
        return remote(
            tot_all.at[col], tot_all.at[col], r["tot_send"].at[step - 1], r["tot_recv"].at[step - 1], row, col_mate(step)
        )

    for step in range(1, cols_n):
        tot(step).start()

    both_parts = jnp.concatenate([high, low], axis=0)
    by_key = contract(both_parts, r["w_key"][...], 1, 1)
    by_value = contract(both_parts, r["w_value"][...], 1, 1)
    grad_normed = by_key[:own] + by_key[2 * own : 3 * own] + by_value[own : 2 * own] + by_value[3 * own :]
    grad_pooled = (
        grad_normed
        - jnp.mean(grad_normed, axis=-1, keepdims=True)
        - standard * jnp.mean(grad_normed * standard, axis=-1, keepdims=True)
    ) * inverse
    grad_pooled = grad_pooled / (POOL * POOL)
    for cell_row in range(height // POOL):
        rows = grad_pooled[cell_row * per_row : (cell_row + 1) * per_row]
        over = jnp.broadcast_to(rows[:, None, :], (per_row, POOL, channels)).reshape(width, channels)
        r["over"][cell_row] = over

    @pl.loop(0, height)
    def _(at):
        pad2[at + 1, middle] = pad2[at + 1, middle] + r["over"][at // POOL]

    send_halo(2)

    r["tap_terms"][...] = jnp.zeros_like(r["tap_terms"])

    @pl.loop(0, channels // LANES)
    def _(part):
        lanes = pl.ds(pl.multiple_of(part * LANES, LANES), LANES)
        sums = [jnp.zeros((8, LANES), F32) for _ in range(9)]
        for at in range(height):
            value = pad2[at + 1, middle, lanes]
            for i in range(9):
                product = value * pad1[at + i // 3, pl.ds(EDGE - 1 + i % 3, width), lanes]
                sums[i] = sums[i] + product.reshape(width // 8, 8, LANES).sum(axis=0)
        for i in range(9):
            r["tap_terms"][i : i + 1, lanes] = sums[i].sum(axis=0, keepdims=True)

    tap_out, tap_in, tap_out2, tap_in2 = r["tap_out"], r["tap_in"], r["tap_out2"], r["tap_in2"]
    tap_out[...] = r["tap_terms"][...].astype(BF16)

    def tap_first(step):
        return remote(tap_out, tap_in.at[step - 1], r["tap_send1"].at[step - 1], r["tap_recv1"].at[step - 1], row_mate(step), col)

    def tap_second(step):
        return remote(tap_out2, tap_in2.at[step - 1], r["tap_send2"].at[step - 1], r["tap_recv2"].at[step - 1], row, col_mate(step))

    for step in range(1, rows_n):
        tap_first(step).start()

    start_third(0)

    for step in range(1, cols_n):
        tot(step).wait()
    is_key = col < 2 * items
    sides = []
    for at in range(cols_n):
        value = tot_all[at].astype(F32)
        sides.append(jnp.where(is_key, value[:own], value[own:]))
    r["side_all"][row] = jnp.concatenate(sides, axis=0).astype(BF16)

    def pass_on(name, step):
        return remote(
            r[name].at[row], r[name].at[row], r[name + "_send"].at[step - 1], r[name + "_recv"].at[step - 1], row_mate(step), col
        )

    @pl.when(is_cells)
    def _():
        for name in ("key_all", "side_all"):
            for step in range(1, rows_n):
                pass_on(name, step).start()

    tap_total = tap_out[...].astype(F32)
    for step in range(1, rows_n):
        tap_first(step).wait()
        tap_total = tap_total + tap_in[step - 1].astype(F32)
    tap_out2[...] = tap_total.astype(BF16)
    for step in range(1, cols_n):
        tap_second(step).start()

    start_third(1)
    wait_edges(2, (True, False))
    take_cols(2)

    @pl.loop(0, channels // LANES)
    def _(part):
        lanes = pl.ds(pl.multiple_of(part * LANES, LANES), LANES)
        weight = [jnp.broadcast_to(taps[i : i + 1, lanes], (width, LANES)) for i in range(9)]
        for at in range(height):
            total = pad2[at + 1, middle, lanes]
            for i in range(9):
                total = total + weight[i] * pad2[at + 2 - i // 3, pl.ds(EDGE + 1 - i % 3, width), lanes]
            r["grad_image"][at, :, lanes] = total.astype(BF16)

    start_fourth(0)
    start_fourth(1)

    tap_total = tap_out2[...].astype(F32)
    for step in range(1, cols_n):
        tap_second(step).wait()
        tap_total = tap_total + tap_in2[step - 1].astype(F32)
    r["tap_sum"][...] = tap_total

    for item in range(items):
        first(item).wait_send()
        for step in range(1, rows_n):
            for sub in range(2):
                second(item, step, sub).wait_send()

        @pl.when(chip != owner_of(item))
        def _(item=item):
            for sub in range(2):
                third(item, sub).wait_send()

    @pl.when(is_terms)
    def _():
        for step in range(1, rows_n):
            for sub in range(2):
                fourth(step, sub).wait()

    @pl.when(is_cells)
    def _():
        for name in ("key_all", "side_all"):
            for step in range(1, rows_n):
                pass_on(name, step).wait()


def on_device(image, conv_taps, w_query, w_key, w_value, w_out, grad_out):
    rows_n, cols_n = lax.axis_size("row"), lax.axis_size("col")
    height, width, channels = image.shape
    tokens = height * width
    own = (height // POOL) * (width // POOL)
    cells_n = cols_n * own
    chips, items = cols_n // 2, cols_n // 4
    shard = 4 * channels // cols_n
    high = channels // rows_n
    operands = dict(
        image=image, grad_out=grad_out.reshape(tokens, channels), taps=conv_taps,
        w_query=w_query, w_key=w_key, w_value=w_value, w_out=w_out,
    )
    shapes = dict(
        grad_image=(image.shape, BF16),
        summed_all=((rows_n, high, shard), BF16),
        key_all=((rows_n, cells_n, channels), BF16),
        side_all=((rows_n, cells_n, channels), BF16),
        tap_sum=((16, channels), F32),
    )
    scratch = dict(
        pad1=((height + 2, width + 2 * EDGE, channels), F32),
        pad2=((height + 2, width + 2 * EDGE, channels), F32),
        edges_out1=((2, height, channels), F32), edges_in1=((2, height, channels), F32),
        edges_out2=((2, height, channels), F32), edges_in2=((2, height, channels), F32),
        rows_in1=((2, width, channels), BF16), corners_in1=((4, 2 * EDGE, channels), BF16),
        hidden=((tokens, channels), BF16), query=((tokens, channels), BF16), dout=((tokens, channels), BF16),
        attended=((tokens, channels), BF16), grad_query=((tokens, channels), BF16),
        pooled=((own, channels), F32), over=((height // POOL, width, channels), F32),
        cellbuf=((cols_n, own, channels), BF16),
        keys=((cells_n, channels), BF16), values=((cells_n, channels), BF16),
        blocks=((cols_n, 2 * own, channels), BF16), blocks_in=((cols_n - 1, 2 * own, channels), BF16),
        tot_all=((cols_n, 2 * own, channels), BF16),
        terms=((2, items, rows_n, high, shard), BF16),
        landed1=((items, rows_n, high, shard), BF16), held1=((items, rows_n, high, shard), BF16),
        landed2=((items, rows_n - 1, high, shard), BF16), held2=((items, high, shard), BF16),
        landed3=((chips, high, shard), BF16),
        tap_terms=((16, channels), F32),
        tap_out=((16, channels), BF16), tap_in=((rows_n - 1, 16, channels), BF16),
        tap_out2=((16, channels), BF16), tap_in2=((cols_n - 1, 16, channels), BF16),
    )
    sems = dict(
        halo_send1=(8,), halo_recv1=(8,), halo_send2=(8,), halo_recv2=(8,),
        cell_send=(cols_n - 1,), cell_recv=(cols_n - 1,),
        block_send=(cols_n - 1,), block_recv=(cols_n - 1,),
        tot_send=(cols_n - 1,), tot_recv=(cols_n - 1,),
        send1=(items,), recv1=(items,), send2=(items, rows_n - 1, 2), recv2=(items, rows_n - 1, 2),
        send3=(items, 2), recv3=(chips, 2), send4=(rows_n - 1, 2), recv4=(rows_n - 1, 2),
        tap_send1=(rows_n - 1,), tap_recv1=(rows_n - 1,),
        tap_send2=(cols_n - 1,), tap_recv2=(cols_n - 1,),
        key_all_send=(rows_n - 1,), key_all_recv=(rows_n - 1,),
        side_all_send=(rows_n - 1,), side_all_recv=(rows_n - 1,),
    )
    names = list(operands) + list(shapes) + list(scratch) + list(sems)
    grad_image, summed_all, key_all, side_all, tap_sum = pl.pallas_call(
        partial(block_kernel, rows_n, cols_n, names),
        out_shape=[jax.ShapeDtypeStruct(*spec) for spec in shapes.values()],
        in_specs=[VMEM] * len(operands),
        out_specs=[VMEM] * len(shapes),
        scratch_shapes=[pltpu.VMEM(*spec) for spec in scratch.values()]
        + [pltpu.SemaphoreType.DMA(spec) for spec in sems.values()],
        compiler_params=pltpu.CompilerParams(
            collective_id=0, has_side_effects=True, vmem_limit_bytes=60 * 2**20
        ),
    )(*operands.values())
    quarter = cols_n // 4
    col = lax.axis_index("col")
    mine = lax.dynamic_slice_in_dim(
        side_all.reshape(-1, channels), lax.rem(col, quarter) * shard, shard, axis=1
    )
    from_cells = contract(key_all.reshape(-1, channels), mine, 0, 0)
    is_cells = jnp.logical_and(col >= quarter, col < cols_n - quarter)
    grad_weights = jnp.where(is_cells, from_cells, summed_all.reshape(channels, shard).astype(F32))
    grad_conv = lax.dynamic_slice_in_dim(
        tap_sum[:9], col * (channels // cols_n), channels // cols_n, axis=1
    )
    return (grad_image, grad_weights, grad_conv)


def solution(mesh):
    return jax.shard_map(
        on_device,
        mesh=mesh,
        in_specs=(P("row", "col", None), P(), P(), P(), P(), P(), P("row", "col", None)),
        out_specs=(P("row", "col", None), P(None, "col"), P(None, "col")),
        check_vma=False,
    )
```

```python
from functools import partial

import jax
import jax.numpy as jnp
from jax import lax
from jax.experimental import pallas as pl
from jax.experimental.pallas import tpu as pltpu
from jax.sharding import PartitionSpec as P

HD = 64
POOL = 8
LANES = 128
EDGE = 8

EPSILON = 1e-05
MESH = pl.DeviceIdType.MESH
VMEM = pl.BlockSpec(memory_space=pltpu.VMEM)
DIRECTIONS = ((-1, 0), (1, 0), (0, -1), (0, 1), (-1, -1), (-1, 1), (1, -1), (1, 1))
F32 = jnp.float32
BF16 = jnp.bfloat16


def contract(left, right, at_left, at_right):
    return lax.dot_general(
        left, right, (((at_left,), (at_right,)), ((), ())), preferred_element_type=F32
    )


def split(value):
    high = value.astype(BF16)
    return high, (value - high.astype(F32)).astype(BF16)


def remote(source, target, send, recv, row, col):
    return pltpu.make_async_remote_copy(
        src_ref=source,
        dst_ref=target,
        send_sem=send,
        recv_sem=recv,
        device_id=(row, col),
        device_id_type=MESH,
    )


def block_kernel(rows_n, cols_n, names, *refs):
    r = dict(zip(names, refs, strict=True))
    image, grad_out, taps = r["image"], r["grad_out"], r["taps"]
    pad1, pad2 = r["pad1"], r["pad2"]
    hidden, query, dout = r["hidden"], r["query"], r["dout"]
    attended, grad_query = r["attended"], r["grad_query"]
    height, width, channels = image.shape
    own = (height // POOL) * (width // POOL)
    per_row = width // POOL
    cells_n = cols_n * own
    shard = r["terms"].shape[4]
    row, col = lax.axis_index("row"), lax.axis_index("col")
    chip, core = col // 2, lax.rem(col, 2)
    chips, items = cols_n // 2, cols_n // 4
    half = items // 2
    is_cells = jnp.logical_and(chip >= half, chip < chips - half)
    is_terms = jnp.logical_or(chip < half, chip >= chips - half)

    def row_mate(step):
        return lax.rem(row + step, rows_n)

    def col_mate(step):
        return lax.rem(col + step, cols_n)

    def present(down, right):
        ok = None
        for move, at, count in ((down, row, rows_n), (right, col, cols_n)):
            if move == 0:
                continue
            here = at > 0 if move < 0 else at < count - 1
            ok = here if ok is None else jnp.logical_and(ok, here)
        return ok

    for at in (0, height + 1):
        pad2[at] = jnp.zeros_like(pad2[at])
    for name in ("edges_in1", "edges_in2", "rows_in1", "corners_in1"):
        r[name][...] = jnp.zeros_like(r[name])

    barrier = pltpu.get_barrier_semaphore()
    greeted = cols_n + rows_n - 2
    for down, right in DIRECTIONS:
        greeted = greeted + present(down, right).astype(jnp.int32)

        @pl.when(present(down, right))
        def _(down=down, right=right):
            pl.semaphore_signal(barrier, inc=1, device_id=(row + down, col + right), device_id_type=MESH)
    for step in range(1, cols_n):
        pl.semaphore_signal(barrier, inc=1, device_id=(row, col_mate(step)), device_id_type=MESH)
    for step in range(1, rows_n):
        pl.semaphore_signal(barrier, inc=1, device_id=(row_mate(step), col), device_id_type=MESH)

    middle = pl.ds(EDGE, width)
    near, far = pl.ds(EDGE, EDGE), pl.ds(width, EDGE)
    before, after = pl.ds(0, EDGE), pl.ds(EDGE + width, EDGE)

    def edge(number, at):
        pad, out, got = (pad1, r["edges_out1"], r["edges_in1"]) if number == 1 else (pad2, r["edges_out2"], r["edges_in2"])
        down, right = DIRECTIONS[at]
        source = 1 if down < 0 else height
        target = height + 1 if down < 0 else 0
        if down == 0:
            source_ref, target_ref = out.at[0 if right < 0 else 1], got.at[1 if right < 0 else 0]
        elif number == 1 and right == 0:
            source_ref, target_ref = image.at[source - 1], r["rows_in1"].at[1 if down < 0 else 0]
        elif number == 1:
            source_ref = image.at[source - 1, pl.ds(0 if right < 0 else width - 2 * EDGE, 2 * EDGE)]
            target_ref = r["corners_in1"].at[(2 if down < 0 else 0) + (1 if right < 0 else 0)]
        elif right == 0:
            source_ref, target_ref = pad.at[source, middle], pad.at[target, middle]
        elif right < 0:
            source_ref, target_ref = pad.at[source, near], pad.at[target, after]
        else:
            source_ref, target_ref = pad.at[source, far], pad.at[target, before]
        return remote(
            source_ref, target_ref, r[f"halo_send{number}"].at[at], r[f"halo_recv{number}"].at[at], row + down, col + right
        )

    def send_halo(number):
        pad, out = (pad1, r["edges_out1"]) if number == 1 else (pad2, r["edges_out2"])
        for at in range(height):
            if number == 1:
                out[0, at : at + 1] = image[at, : 2 * EDGE].astype(F32)[:1]
                out[1, at : at + 1] = image[at, width - 2 * EDGE :].astype(F32)[2 * EDGE - 1 :]
            else:
                out[0, at : at + 1] = pad[at + 1, EDGE : EDGE + 1]
                out[1, at : at + 1] = pad[at + 1, EDGE + width - 1 : EDGE + width]
        if number == 1:
            pl.semaphore_wait(barrier, greeted)
        for at, (down, right) in enumerate(DIRECTIONS):
            @pl.when(present(down, right))
            def _(at=at):
                edge(number, at).start()

    def wait_edges(number, wanted):
        for at, (down, right) in enumerate(DIRECTIONS):
            if (down == 0) not in wanted:
                continue

            @pl.when(present(-down, -right))
            def _(at=at):
                edge(number, at).wait_recv()

            @pl.when(present(down, right))
            def _(at=at):
                edge(number, at).wait_send()

    def take_cols(number):
        pad, got = (pad1, r["edges_in1"]) if number == 1 else (pad2, r["edges_in2"])
        for at in range(height):
            pad[at + 1, EDGE - 1 : EDGE] = got[0, at : at + 1]
            pad[at + 1, EDGE + width : EDGE + width + 1] = got[1, at : at + 1]

    send_halo(1)

    @pl.loop(0, height)
    def _(at):
        pad1[at + 1, middle] = image[at].astype(F32)

    tokens = height * width
    chunk = tokens // 2

    @pl.loop(0, 2)
    def _(at):
        rows = pl.ds(pl.multiple_of(at * chunk, chunk), chunk)
        dout[rows] = contract(grad_out[rows], r["w_out"][...], 1, 1).astype(BF16)

    def mix(wanted, begin):
        @pl.loop(0, channels // LANES)
        def _(part):
            lanes = pl.ds(pl.multiple_of(part * LANES, LANES), LANES)
            weight = [jnp.broadcast_to(taps[i : i + 1, lanes], (width, LANES)) for i in range(9)]
            for cell_row in range(height // POOL):
                pooled = jnp.zeros((width, LANES), F32)
                some = False
                for at in range(cell_row * POOL, (cell_row + 1) * POOL):
                    if at not in wanted:
                        continue
                    some = True
                    total = jnp.zeros((width, LANES), F32)
                    for i in range(9):
                        total = total + weight[i] * pad1[at + i // 3, pl.ds(EDGE - 1 + i % 3, width), lanes]
                    value = (pad1[at + 1, middle, lanes] + total).astype(BF16)
                    hidden[at * width : (at + 1) * width, lanes] = value
                    pooled = pooled + value.astype(F32)
                if some:
                    where = slice(cell_row * per_row, (cell_row + 1) * per_row)
                    sums = pooled.reshape(per_row, POOL, LANES).sum(axis=1) / (POOL * POOL)
                    r["pooled"][where, lanes] = sums if begin else r["pooled"][where, lanes] + sums

    wait_edges(1, (True,))
    take_cols(1)
    mix(range(1, height - 1), True)
    wait_edges(1, (False,))
    for at, side in ((0, 0), (height + 1, 1)):
        pad1[at, middle] = r["rows_in1"][side].astype(F32)
        pad1[at, EDGE - 1 : EDGE] = r["corners_in1"][2 * side].astype(F32)[2 * EDGE - 1 :]
        pad1[at, EDGE + width : EDGE + width + 1] = r["corners_in1"][2 * side + 1].astype(F32)[:1]
    mix((0, height - 1), False)

    pooled = r["pooled"][...]
    centre = jnp.mean(pooled, axis=-1, keepdims=True)
    spread = jnp.mean(jnp.square(pooled - centre), axis=-1, keepdims=True)
    inverse = lax.rsqrt(spread + EPSILON)
    standard = (pooled - centre) * inverse
    cellbuf = r["cellbuf"]
    cellbuf[col] = standard.astype(BF16)

    def cell(step):
        return remote(
            cellbuf.at[col], cellbuf.at[col], r["cell_send"].at[step - 1], r["cell_recv"].at[step - 1], row, col_mate(step)
        )

    for step in range(1, cols_n):
        cell(step).start()

    @pl.loop(0, 2)
    def _(at):
        rows = pl.ds(pl.multiple_of(at * chunk, chunk), chunk)
        query[rows] = contract(hidden[rows], r["w_query"][...], 1, 0).astype(BF16)

    for step in range(1, cols_n):
        cell(step).wait()
    key_cells = jnp.concatenate([cellbuf[at].astype(F32) for at in range(cols_n)], axis=0).astype(BF16)
    r["key_all"][row] = key_cells
    r["keys"][...] = contract(key_cells, r["w_key"][...], 1, 0).astype(BF16)
    r["values"][...] = contract(key_cells, r["w_value"][...], 1, 0).astype(BF16)

    pair_cells = 2 * cells_n
    same_head = (
        lax.broadcasted_iota(jnp.int32, (pair_cells, LANES), 0) // cells_n
        == lax.broadcasted_iota(jnp.int32, (pair_cells, LANES), 1) // HD
    )
    cell_ones = (
        lax.broadcasted_iota(jnp.int32, (pair_cells, pair_cells), 0) // cells_n
        == lax.broadcasted_iota(jnp.int32, (pair_cells, pair_cells), 1) // cells_n
    ).astype(F32).astype(BF16)
    lane_ones = (
        lax.broadcasted_iota(jnp.int32, (LANES, pair_cells), 0) // HD
        == lax.broadcasted_iota(jnp.int32, (LANES, pair_cells), 1) // cells_n
    ).astype(F32).astype(BF16)
    first_head = lax.broadcasted_iota(jnp.int32, (cells_n, LANES), 1) < HD
    scale = HD ** (-0.5)

    def summed(value, ones):
        high, low = split(value)
        return contract(high, ones, 1, 0) + contract(low, ones, 1, 0)

    @pl.loop(0, channels // LANES)
    def _(part):
        lanes = pl.ds(pl.multiple_of(part * LANES, LANES), LANES)

        def both(ref):
            value = ref[:, lanes].astype(F32)
            twice = jnp.concatenate([value, value], axis=0)
            return jnp.where(same_head, twice, 0.0).astype(BF16)

        key_pair, value_pair = both(r["keys"]), both(r["values"])
        queries, douts = query[:, lanes], dout[:, lanes]
        expons = jnp.exp(contract(queries, key_pair, 1, 1) * scale)
        probabilities = expons / summed(expons, cell_ones)
        weights = probabilities.astype(BF16)
        got = contract(weights, value_pair, 1, 0).astype(BF16)
        attended[:, lanes] = got
        grad_probs = contract(douts, value_pair, 1, 1)
        deltas = summed(douts.astype(F32) * got.astype(F32), lane_ones)
        grad_scores = (probabilities * (grad_probs - deltas) * scale).astype(BF16)
        grad_query[:, lanes] = contract(grad_scores, key_pair, 1, 0).astype(BF16)
        grad_key = contract(grad_scores, queries, 0, 0)
        grad_value = contract(weights, douts, 0, 0)
        grad_key = jnp.where(first_head, grad_key[:cells_n], grad_key[cells_n:])
        grad_value = jnp.where(first_head, grad_value[:cells_n], grad_value[cells_n:])
        for owner in range(cols_n):
            rows = slice(owner * own, (owner + 1) * own)
            r["blocks"][owner, :, lanes] = jnp.concatenate([grad_key[rows], grad_value[rows]], axis=0).astype(BF16)

    def block(step):
        owner = col_mate(step)
        return remote(
            r["blocks"].at[owner], r["blocks_in"].at[step - 1], r["block_send"].at[step - 1], r["block_recv"].at[step - 1], row, owner
        )

    for step in range(1, cols_n):
        block(step).start()

    terms, landed1, held1 = r["terms"], r["landed1"], r["held1"]
    landed2, held2, landed3, summed_all = r["landed2"], r["held2"], r["landed3"], r["summed_all"]

    def first(item):
        return remote(
            terms.at[1 - core, item], landed1.at[item], r["send1"].at[item], r["recv1"].at[item], row, 2 * chip + 1 - core
        )

    deep = terms.shape[3] // 2
    part_of = [pl.ds(sub * deep, deep) for sub in range(2)]

    def second(item, step, sub):
        return remote(
            held1.at[item, row_mate(step), part_of[sub]], landed2.at[item, step - 1, part_of[sub]],
            r["send2"].at[item, step - 1, sub], r["recv2"].at[item, step - 1, sub], row_mate(step), col,
        )

    def owner_of(item):
        return item if item < half else chips - items + item

    def third(item, sub):
        return remote(
            held2.at[item, part_of[sub]], landed3.at[chip, part_of[sub]], r["send3"].at[item, sub],
            r["recv3"].at[chip, sub], row, 2 * owner_of(item) + core,
        )

    def fourth(step, sub):
        return remote(
            summed_all.at[row, part_of[sub]], summed_all.at[row, part_of[sub]], r["send4"].at[step - 1, sub],
            r["recv4"].at[step - 1, sub], row_mate(step), col,
        )

    def start_second():
        for sub in range(2):
            for item in range(items):
                if sub == 0:
                    first(item).wait_recv()
                for step in range(1, rows_n + 1):
                    there = row_mate(step)
                    held1[item, there, part_of[sub]] = (
                        terms[core, item, there, part_of[sub]].astype(F32)
                        + landed1[item, there, part_of[sub]].astype(F32)
                    ).astype(BF16)
                    if step < rows_n:
                        second(item, step, sub).start()

    def start_third(sub):
        for item in range(items):
            total = held1[item, row, part_of[sub]].astype(F32)
            for step in range(1, rows_n):
                second(item, step, sub).wait_recv()
                total = total + landed2[item, step - 1, part_of[sub]].astype(F32)
            held2[item, part_of[sub]] = total.astype(BF16)

            @pl.when(chip != owner_of(item))
            def _(item=item):
                third(item, sub).start()

    def start_fourth(sub):
        @pl.when(is_terms)
        def _():
            mine = lax.rem(chip, chips - items)
            total = held2[mine, part_of[sub]].astype(F32)
            for step in range(1, chips):
                source = lax.rem(chip + step, chips)
                remote(
                    held2.at[0, part_of[sub]], landed3.at[source, part_of[sub]], r["send3"].at[0, sub],
                    r["recv3"].at[source, sub], row, 2 * source + core,
                ).wait_recv()
                total = total + landed3[source, part_of[sub]].astype(F32)
            summed_all[row, part_of[sub]] = total.astype(BF16)
            for step in range(1, rows_n):
                fourth(step, sub).start()

    for left, right, begin in ((hidden, grad_query, 0), (attended, grad_out, half)):
        for item in range(half):
            for side in range(2):
                at = (2 * item + side) * shard
                term = contract(left[...], right[:, at : at + shard], 0, 0).astype(BF16)
                terms[side, begin + item] = term.reshape(terms.shape[2:])
            first(begin + item).start()

    @pl.loop(0, 2)
    def _(at):
        rows = pl.ds(pl.multiple_of(at * chunk, chunk), chunk)
        value = contract(grad_query[rows], r["w_query"][...], 1, 1) + grad_out[rows].astype(F32)
        pad2[pl.ds(1 + at * (height // 2), height // 2), middle] = value.reshape(height // 2, width, channels)

    start_second()

    totals = r["blocks"][col].astype(F32)
    for step in range(1, cols_n):
        block(step).wait()
        totals = totals + r["blocks_in"][step - 1].astype(F32)
    high, low = split(totals)
    tot_all = r["tot_all"]
    tot_all[col] = high

    def tot(step):
        return remote(
            tot_all.at[col], tot_all.at[col], r["tot_send"].at[step - 1], r["tot_recv"].at[step - 1], row, col_mate(step)
        )

    for step in range(1, cols_n):
        tot(step).start()

    both_parts = jnp.concatenate([high, low], axis=0)
    by_key = contract(both_parts, r["w_key"][...], 1, 1)
    by_value = contract(both_parts, r["w_value"][...], 1, 1)
    grad_normed = by_key[:own] + by_key[2 * own : 3 * own] + by_value[own : 2 * own] + by_value[3 * own :]
    grad_pooled = (
        grad_normed
        - jnp.mean(grad_normed, axis=-1, keepdims=True)
        - standard * jnp.mean(grad_normed * standard, axis=-1, keepdims=True)
    ) * inverse
    grad_pooled = grad_pooled / (POOL * POOL)
    for cell_row in range(height // POOL):
        rows = grad_pooled[cell_row * per_row : (cell_row + 1) * per_row]
        over = jnp.broadcast_to(rows[:, None, :], (per_row, POOL, channels)).reshape(width, channels)
        r["over"][cell_row] = over

    @pl.loop(0, height)
    def _(at):
        pad2[at + 1, middle] = pad2[at + 1, middle] + r["over"][at // POOL]

    send_halo(2)

    r["tap_terms"][...] = jnp.zeros_like(r["tap_terms"])

    @pl.loop(0, channels // LANES)
    def _(part):
        lanes = pl.ds(pl.multiple_of(part * LANES, LANES), LANES)
        sums = [jnp.zeros((8, LANES), F32) for _ in range(9)]
        for at in range(height):
            value = pad2[at + 1, middle, lanes]
            for i in range(9):
                product = value * pad1[at + i // 3, pl.ds(EDGE - 1 + i % 3, width), lanes]
                sums[i] = sums[i] + product.reshape(width // 8, 8, LANES).sum(axis=0)
        for i in range(9):
            r["tap_terms"][i : i + 1, lanes] = sums[i].sum(axis=0, keepdims=True)

    tap_out, tap_in, tap_out2, tap_in2 = r["tap_out"], r["tap_in"], r["tap_out2"], r["tap_in2"]
    tap_out[...] = r["tap_terms"][...].astype(BF16)

    def tap_first(step):
        return remote(tap_out, tap_in.at[step - 1], r["tap_send1"].at[step - 1], r["tap_recv1"].at[step - 1], row_mate(step), col)

    def tap_second(step):
        return remote(tap_out2, tap_in2.at[step - 1], r["tap_send2"].at[step - 1], r["tap_recv2"].at[step - 1], row, col_mate(step))

    for step in range(1, rows_n):
        tap_first(step).start()

    start_third(0)

    for step in range(1, cols_n):
        tot(step).wait()
    is_key = col < 2 * items
    sides = []
    for at in range(cols_n):
        value = tot_all[at].astype(F32)
        sides.append(jnp.where(is_key, value[:own], value[own:]))
    r["side_all"][row] = jnp.concatenate(sides, axis=0).astype(BF16)

    def pass_on(name, step):
        return remote(
            r[name].at[row], r[name].at[row], r[name + "_send"].at[step - 1], r[name + "_recv"].at[step - 1], row_mate(step), col
        )

    @pl.when(is_cells)
    def _():
        for name in ("key_all", "side_all"):
            for step in range(1, rows_n):
                pass_on(name, step).start()

    tap_total = tap_out[...].astype(F32)
    for step in range(1, rows_n):
        tap_first(step).wait()
        tap_total = tap_total + tap_in[step - 1].astype(F32)
    tap_out2[...] = tap_total.astype(BF16)
    for step in range(1, cols_n):
        tap_second(step).start()

    def unmix(wanted):
        @pl.loop(0, channels // LANES)
        def _(part):
            lanes = pl.ds(pl.multiple_of(part * LANES, LANES), LANES)
            weight = [jnp.broadcast_to(taps[i : i + 1, lanes], (width, LANES)) for i in range(9)]
            for at in wanted:
                total = pad2[at + 1, middle, lanes]
                for i in range(9):
                    total = total + weight[i] * pad2[at + 2 - i // 3, pl.ds(EDGE + 1 - i % 3, width), lanes]
                r["grad_image"][at, :, lanes] = total.astype(BF16)

    wait_edges(2, (True,))
    take_cols(2)
    unmix(range(1, height - 1))
    start_third(1)
    wait_edges(2, (False,))
    unmix((0, height - 1))

    start_fourth(0)
    start_fourth(1)

    tap_total = tap_out2[...].astype(F32)
    for step in range(1, cols_n):
        tap_second(step).wait()
        tap_total = tap_total + tap_in2[step - 1].astype(F32)
    r["tap_sum"][...] = tap_total

    for item in range(items):
        first(item).wait_send()
        for step in range(1, rows_n):
            for sub in range(2):
                second(item, step, sub).wait_send()

        @pl.when(chip != owner_of(item))
        def _(item=item):
            for sub in range(2):
                third(item, sub).wait_send()

    @pl.when(is_terms)
    def _():
        for step in range(1, rows_n):
            for sub in range(2):
                fourth(step, sub).wait()

    @pl.when(is_cells)
    def _():
        for name in ("key_all", "side_all"):
            for step in range(1, rows_n):
                pass_on(name, step).wait()


def on_device(image, conv_taps, w_query, w_key, w_value, w_out, grad_out):
    rows_n, cols_n = lax.axis_size("row"), lax.axis_size("col")
    height, width, channels = image.shape
    tokens = height * width
    own = (height // POOL) * (width // POOL)
    cells_n = cols_n * own
    chips, items = cols_n // 2, cols_n // 4
    shard = 4 * channels // cols_n
    high = channels // rows_n
    operands = dict(
        image=image, grad_out=grad_out.reshape(tokens, channels), taps=conv_taps,
        w_query=w_query, w_key=w_key, w_value=w_value, w_out=w_out,
    )
    shapes = dict(
        grad_image=(image.shape, BF16),
        summed_all=((rows_n, high, shard), BF16),
        key_all=((rows_n, cells_n, channels), BF16),
        side_all=((rows_n, cells_n, channels), BF16),
        tap_sum=((16, channels), F32),
    )
    scratch = dict(
        pad1=((height + 2, width + 2 * EDGE, channels), F32),
        pad2=((height + 2, width + 2 * EDGE, channels), F32),
        edges_out1=((2, height, channels), F32), edges_in1=((2, height, channels), F32),
        edges_out2=((2, height, channels), F32), edges_in2=((2, height, channels), F32),
        rows_in1=((2, width, channels), BF16), corners_in1=((4, 2 * EDGE, channels), BF16),
        hidden=((tokens, channels), BF16), query=((tokens, channels), BF16), dout=((tokens, channels), BF16),
        attended=((tokens, channels), BF16), grad_query=((tokens, channels), BF16),
        pooled=((own, channels), F32), over=((height // POOL, width, channels), F32),
        cellbuf=((cols_n, own, channels), BF16),
        keys=((cells_n, channels), BF16), values=((cells_n, channels), BF16),
        blocks=((cols_n, 2 * own, channels), BF16), blocks_in=((cols_n - 1, 2 * own, channels), BF16),
        tot_all=((cols_n, 2 * own, channels), BF16),
        terms=((2, items, rows_n, high, shard), BF16),
        landed1=((items, rows_n, high, shard), BF16), held1=((items, rows_n, high, shard), BF16),
        landed2=((items, rows_n - 1, high, shard), BF16), held2=((items, high, shard), BF16),
        landed3=((chips, high, shard), BF16),
        tap_terms=((16, channels), F32),
        tap_out=((16, channels), BF16), tap_in=((rows_n - 1, 16, channels), BF16),
        tap_out2=((16, channels), BF16), tap_in2=((cols_n - 1, 16, channels), BF16),
    )
    sems = dict(
        halo_send1=(8,), halo_recv1=(8,), halo_send2=(8,), halo_recv2=(8,),
        cell_send=(cols_n - 1,), cell_recv=(cols_n - 1,),
        block_send=(cols_n - 1,), block_recv=(cols_n - 1,),
        tot_send=(cols_n - 1,), tot_recv=(cols_n - 1,),
        send1=(items,), recv1=(items,), send2=(items, rows_n - 1, 2), recv2=(items, rows_n - 1, 2),
        send3=(items, 2), recv3=(chips, 2), send4=(rows_n - 1, 2), recv4=(rows_n - 1, 2),
        tap_send1=(rows_n - 1,), tap_recv1=(rows_n - 1,),
        tap_send2=(cols_n - 1,), tap_recv2=(cols_n - 1,),
        key_all_send=(rows_n - 1,), key_all_recv=(rows_n - 1,),
        side_all_send=(rows_n - 1,), side_all_recv=(rows_n - 1,),
    )
    names = list(operands) + list(shapes) + list(scratch) + list(sems)
    grad_image, summed_all, key_all, side_all, tap_sum = pl.pallas_call(
        partial(block_kernel, rows_n, cols_n, names),
        out_shape=[jax.ShapeDtypeStruct(*spec) for spec in shapes.values()],
        in_specs=[VMEM] * len(operands),
        out_specs=[VMEM] * len(shapes),
        scratch_shapes=[pltpu.VMEM(*spec) for spec in scratch.values()]
        + [pltpu.SemaphoreType.DMA(spec) for spec in sems.values()],
        compiler_params=pltpu.CompilerParams(
            collective_id=0, has_side_effects=True, vmem_limit_bytes=60 * 2**20
        ),
    )(*operands.values())
    quarter = cols_n // 4
    col = lax.axis_index("col")
    mine = lax.dynamic_slice_in_dim(
        side_all.reshape(-1, channels), lax.rem(col, quarter) * shard, shard, axis=1
    )
    from_cells = contract(key_all.reshape(-1, channels), mine, 0, 0)
    is_cells = jnp.logical_and(col >= quarter, col < cols_n - quarter)
    grad_weights = jnp.where(is_cells, from_cells, summed_all.reshape(channels, shard).astype(F32))
    grad_conv = lax.dynamic_slice_in_dim(
        tap_sum[:9], col * (channels // cols_n), channels // cols_n, axis=1
    )
    return (grad_image, grad_weights, grad_conv)


def solution(mesh):
    return jax.shard_map(
        on_device,
        mesh=mesh,
        in_specs=(P("row", "col", None), P(), P(), P(), P(), P(), P("row", "col", None)),
        out_specs=(P("row", "col", None), P(None, "col"), P(None, "col")),
        check_vma=False,
    )
```
